32 devices in a mesh: grp: 2 (over y), inp: 4 (over z), tm: 2 (over x), pol: 2 (over core).
Axes of the slice: x: 2, y: 2, z: 4, core: 2. Of those that a mesh axis runs over, the one named last changes fastest.
Arguments:
- samples: bfloat16 [512, 64, 4096], P(('grp', 'inp'), ('tm', 'pol')), parts along dimension 0, may hold values from -6 to 6
- coefficients: float32 [16, 4096], replicated, may hold values from -1.5 to 1.5
Outputs:
- visibilities: float32 [4096, 256, 256], P(('grp', 'inp', 'tm', 'pol')), parts along dimension 0
The draws below stay inside these ranges and needn't reach their ends.
There are 2 independent parts, one for each index of `grp`. The reference program is written for one: setup_inputs(seed, part) draws one part's arguments, and reference() takes and returns one part's arrays. A program takes and returns all parts, laid end to end along the dimension named above; an argument that names none is the same for every part. Nothing has to cross between parts.
All inputs are finite; a program needn't handle non-finite values.
Results may differ from the reference program's by a relative error of at most 0.0034.
Values may be sent and summed in bfloat16 or wider, within the bound.
No kernel may reach another device: no remote copies, remote signals or barrier semaphores. Data moves between devices by JAX's collectives and lax.ppermute only.
A program may use at most 256 MiB of HBM per device.

```python
import math
import jax
import jax.numpy as jnp
from jax import lax

INPUTS = 256
SAMPLES = 4096
TAPS = 16
FRAMES = 64


def block_levels(stream_key, shape, pieces, least, largest):
    def one(position, parts):
        steps = jax.random.uniform(jax.random.fold_in(jax.random.fold_in(stream_key, 6), position), (parts,), jnp.float32, least / len(pieces), largest / len(pieces))
        return jnp.repeat(jnp.exp(steps), shape[position] // parts).reshape((-1,) + (1,) * (len(shape) - position - 1))

    level = one(*pieces[0])
    for cut in pieces[1:]:
        level = level * one(*cut)
    return level


def bell_draw(key, shape, scale, limit, split=(), held_as=jnp.bfloat16):
    array = jax.random.normal(key, shape, jnp.float32) * scale
    if len(split) > 0:
        array = block_levels(key, shape, split, -0.22, 0.18) * array
    return jnp.clip(array, min=-limit, max=limit).astype(held_as)


def setup_inputs(seed: int = 0, part: int = 0) -> dict:
    splits = jax.random.split(jax.random.key(seed), 3)
    own_keys = jax.random.split(jax.random.fold_in(splits[2], part), 3)
    samples = bell_draw(own_keys[0], (INPUTS, FRAMES, SAMPLES), 1.0, 6.0, ((0, 4), (1, 4)))
    coefficients = bell_draw(splits[1], (TAPS, SAMPLES), 0.25, 1.5, (), jnp.float32)
    return dict(samples=samples, coefficients=coefficients)


def correlate(real_part, imag_part, total_frames):
    joined = jnp.concatenate([real_part, imag_part], axis=2)
    turned = jnp.concatenate([imag_part, -real_part], axis=2)
    stacked = jnp.concatenate([joined, turned], axis=1)
    product = jnp.einsum('cif,cjf->cij', stacked, joined, precision=lax.Precision.HIGHEST)
    width = real_part.shape[1]
    row_index = lax.broadcasted_iota(jnp.int32, (width, width), 0)
    col_index = lax.broadcasted_iota(jnp.int32, (width, width), 1)
    packed = jnp.where(row_index <= col_index, product[:, :width], product[:, width:])
    return packed * (1.0 / total_frames)

def reference(samples, coefficients):
    inputs_all, frames_all, length = samples.shape
    taps = coefficients.shape[0]
    channels = length // 2
    block_inputs = 16
    grouped = samples.reshape(inputs_all // block_inputs, block_inputs, frames_all, length)

    def spectra_of(block):
        padded = jnp.concatenate([jnp.zeros((block_inputs, taps - 1, length), block.dtype), block], axis=1)
        filtered = jnp.zeros((block_inputs, frames_all, length), jnp.float32)
        for tap_index in range(taps):
            filtered = filtered + coefficients[tap_index] * padded[:, tap_index:tap_index + frames_all].astype(jnp.float32)
        spectrum = jnp.fft.rfft(filtered, axis=-1)[..., :channels] / math.sqrt(length)
        return jnp.stack([jnp.real(spectrum), jnp.imag(spectrum)]).astype(jnp.bfloat16)
    spectra = lax.map(spectra_of, grouped)
    band = 64

    def band_of(band_index):
        piece = lax.dynamic_slice_in_dim(spectra, band_index * band, band, 4)
        piece = jnp.transpose(piece, (1, 4, 0, 2, 3)).reshape(2, band, inputs_all, frames_all).astype(jnp.float32)
        return correlate(piece[0], piece[1], frames_all)
    result = lax.map(band_of, jnp.arange(channels // band, dtype=jnp.int32))
    return result.reshape(channels, inputs_all, inputs_all)
```

```python
import functools
import math

import jax
import jax.numpy as jnp
import ml_dtypes
import numpy as np
from jax import lax
from jax.experimental import pallas as pl
from jax.experimental.pallas import tpu as pltpu
from jax.sharding import PartitionSpec as P

RADIX = 16
GROUPS = RADIX // 2
LANES = 128
ROWS = 8
MIB = 1 << 20


def from_behind(block, axis, distance):
    devices = range(lax.axis_size(axis))
    route = [(i - distance, i) for i in devices if i - distance in devices]
    return lax.ppermute(block, axis, route)


def correlate(real_part, imag_part, total_frames):
    joined = jnp.concatenate([real_part, imag_part], axis=2)
    turned = jnp.concatenate([imag_part, -real_part], axis=2)
    stacked = jnp.concatenate([joined, turned], axis=1)
    product = jnp.einsum("cif,cjf->cij", stacked, joined, preferred_element_type=jnp.float32)
    width = real_part.shape[1]
    row_index = lax.broadcasted_iota(jnp.int32, (width, width), 0)
    col_index = lax.broadcasted_iota(jnp.int32, (width, width), 1)
    packed = jnp.where(row_index <= col_index, product[:, :width], product[:, width:])
    return packed * (1.0 / total_frames)


def filter_frames(block, coefficients, taps):
    frame_count = block.shape[1] - taps + 1
    total = jnp.zeros((block.shape[0], frame_count, block.shape[2]), jnp.float32)
    for tap_index in range(taps):
        total = total + coefficients[tap_index] * block[
            :, tap_index : tap_index + frame_count
        ].astype(jnp.float32)
    return total


def angles(first_idx, second_idx, period):
    product = first_idx[:, None] * second_idx[None, :] % period
    return product.astype(jnp.float32) * (2.0 * math.pi / period)


def transform(filtered):
    row_total, length = filtered.shape
    inner_len = 2 ** ((length.bit_length() - 1) // 2)
    outer_len = length // inner_len
    blocks = filtered.reshape(row_total, inner_len, outer_len)
    inner_idx = jnp.arange(inner_len, dtype=jnp.int32)
    outer_idx = jnp.arange(outer_len, dtype=jnp.int32)
    half_idx = jnp.arange(outer_len // 2, dtype=jnp.int32)
    angle_one = angles(inner_idx, inner_idx, inner_len)
    table_one = jnp.concatenate([jnp.cos(angle_one), -jnp.sin(angle_one)], axis=1)
    section_one = jnp.einsum("rab,ak->rbk", blocks, table_one, precision=lax.Precision.HIGHEST)
    first_re = section_one[..., :inner_len]
    first_im = section_one[..., inner_len:]
    angle_twist = angles(outer_idx, inner_idx, length)
    twist_cos = jnp.cos(angle_twist)
    twist_sin = jnp.sin(angle_twist)
    turned_re = first_re * twist_cos + first_im * twist_sin
    turned_im = first_im * twist_cos - first_re * twist_sin
    angle_two = angles(outer_idx, half_idx, outer_len)
    table_cos = jnp.cos(angle_two)
    table_sin = jnp.sin(angle_two)
    highest = lax.Precision.HIGHEST
    out_re = jnp.einsum("rbk,bq->qkr", turned_re, table_cos, precision=highest) + jnp.einsum(
        "rbk,bq->qkr", turned_im, table_sin, precision=highest
    )
    out_im = jnp.einsum("rbk,bq->qkr", turned_im, table_cos, precision=highest) - jnp.einsum(
        "rbk,bq->qkr", turned_re, table_sin, precision=highest
    )
    scale_factor = 1.0 / math.sqrt(length)
    return jnp.stack([out_re, out_im]).reshape(2, length // 2, row_total) * scale_factor


def general(samples, coefficients):
    in_dev, frame_count, length = samples.shape
    taps = coefficients.shape[0]
    channels = length // 2
    history = from_behind(samples[:, frame_count - taps + 1 :, :], ("tm", "pol"), 1)
    extended = jnp.concatenate([history, samples], axis=1)
    group_size = math.gcd(in_dev, 4)
    spectra_buf = jnp.zeros((2, channels, in_dev, frame_count), jnp.bfloat16)

    def one_group(group_index, buffer_now):
        block = lax.dynamic_slice_in_dim(extended, group_index * group_size, group_size, 0)
        filtered = filter_frames(block, coefficients, taps).reshape(
            group_size * frame_count, length
        )
        spectra_grp = (
            transform(filtered).reshape(2, channels, group_size, frame_count).astype(jnp.bfloat16)
        )
        return lax.dynamic_update_slice_in_dim(buffer_now, spectra_grp, group_index * group_size, 2)

    local_spec = lax.fori_loop(0, in_dev // group_size, one_group, spectra_buf)
    n_inputs = lax.axis_size("inp")
    n_blocks = lax.axis_size("tm")
    n_halves = lax.axis_size("pol")
    total_frames = frame_count * n_blocks * n_halves
    arrived = lax.all_to_all(
        local_spec[None], ("inp", "tm", "pol"), split_axis=2, concat_axis=0, tiled=True
    )
    width = arrived.shape[2]
    arrived = arrived.reshape(n_inputs, n_blocks * n_halves, 2, width, in_dev, frame_count)
    arrived = jnp.transpose(arrived, (2, 3, 0, 4, 1, 5)).reshape(
        2, width, n_inputs * in_dev, n_blocks * n_halves * frame_count
    )
    return correlate(arrived[0], arrived[1], total_frames)


@functools.lru_cache(maxsize=None)
def fourier_tables(length, owners):
    span = length // RADIX
    per_owner = length // 2 // owners // RADIX
    run = 2 * per_owner
    slots = LANES // run
    place = np.arange(span, dtype=np.int64)
    tables = np.zeros((GROUPS, 2 * span, 2 * owners * run))
    for group in range(GROUPS):
        for owner in range(owners):
            block, inside = divmod(owner, slots)
            column = block * LANES + ((inside - group) % slots) * run
            for side in range(2):
                residue = side * GROUPS if group == 0 else (group, RADIX - group)[side]
                channel = RADIX * (owner * per_owner + np.arange(per_owner)) + residue
                angle = 2.0 * np.pi * (place[:, None] * channel[None, :] % length) / length
                cos, sin = np.cos(angle) / math.sqrt(length), np.sin(angle) / math.sqrt(length)
                re = slice(column + side * per_owner, column + (side + 1) * per_owner)
                im = slice(re.start + owners * run, re.stop + owners * run)
                if group == 0:
                    rows = slice(side * span, (side + 1) * span)
                    tables[group, rows, re] = cos
                    tables[group, rows, im] = -sin
                else:
                    sign = 1.0 - 2.0 * side
                    tables[group, :span, re] = cos
                    tables[group, span:, re] = sign * sin
                    tables[group, :span, im] = -sin
                    tables[group, span:, im] = sign * cos
    exact = tables.astype(np.float32)
    high = exact.astype(ml_dtypes.bfloat16)
    low = (exact - high.astype(np.float32)).astype(ml_dtypes.bfloat16)
    return np.stack([high, low], axis=1)


def real_fourier(values):
    count = len(values)
    if count == 1:
        return [(values[0], None)]
    if count == 2:
        return [(values[0] + values[1], None), (values[0] - values[1], None)]
    even, odd = real_fourier(values[0::2]), real_fourier(values[1::2])
    bins = [None] * (count // 2 + 1)
    bins[0] = (even[0][0] + odd[0][0], None)
    bins[count // 2] = (even[0][0] - odd[0][0], None)
    bins[count // 4] = (even[count // 4][0], -odd[count // 4][0])
    for k in range(1, count // 4):
        (er, ei), (pr, pi) = even[k], odd[k]
        if 8 * k == count:
            half = math.sqrt(0.5)
            tr, ti = (pr + pi) * half, (pi - pr) * half
        else:
            c, s = math.cos(2 * math.pi * k / count), math.sin(2 * math.pi * k / count)
            tr, ti = pr * c + pi * s, pi * c - pr * s
        bins[k] = (er + tr, ei + ti)
        bins[count // 2 - k] = (er - tr, ti - ei)
    return bins


def filter_bank_kernel(
    steps, own_ref, old_ref, coef_ref, table_hbm, out_ref, frames_ref, kept_ref, high_ref, low_ref, spec_ref, table_ref, sem
):
    inputs, frames, length = own_ref.shape
    taps = coef_ref.shape[0]
    span = length // RADIX
    parts = span // LANES
    step = pl.program_id(0)
    copy = pltpu.make_async_copy(table_hbm, table_ref, sem)

    @pl.when(step == 0)
    def _():
        copy.start()

    base = step * inputs * frames

    def one_block(block, carry):
        lanes = pl.ds(pl.multiple_of(block * LANES, LANES), LANES)
        for i in range(inputs):
            frames_ref[pl.ds(2 * frames * i, frames), :] = old_ref[i, :, lanes].astype(jnp.float32)
            frames_ref[pl.ds(2 * frames * i + frames, frames), :] = own_ref[i, :, lanes].astype(jnp.float32)
        taps_now = [jnp.broadcast_to(coef_ref[t : t + 1, lanes], (ROWS, LANES)) for t in range(taps)]
        first = frames - taps + 1
        totals = [None] * frames
        for row in range(first, 2 * frames):
            value = frames_ref[pl.ds(row, inputs, stride=2 * frames), :]
            for f in range(max(0, row - first - taps + 1), min(frames, row - first + 1)):
                term = taps_now[row - first - f] * value
                totals[f] = term if totals[f] is None else totals[f] + term
        for f in range(frames):
            kept_ref[block, pl.ds(f, inputs, stride=frames), :] = totals[f]
        return carry

    lax.fori_loop(0, length // LANES, one_block, 0)

    def one_rows(index, carry):
        part = index % parts
        first = pl.multiple_of(index // parts * 16, 16)
        values = [kept_ref[parts * j + part, pl.ds(first, 16), :] for j in range(RADIX)]
        bins = real_fourier(values)
        rows = pl.ds(pl.multiple_of(base + first, 16), 16)
        for group in range(GROUPS):
            pair = (bins[0][0], bins[GROUPS][0]) if group == 0 else bins[group]
            for half in range(2):
                lanes = pl.ds(pl.multiple_of(half * span + part * LANES, LANES), LANES)
                top = pair[half].astype(jnp.bfloat16)
                high_ref[group, rows, lanes] = top
                low_ref[group, rows, lanes] = (pair[half] - top.astype(jnp.float32)).astype(jnp.bfloat16)
        return carry

    lax.fori_loop(0, parts * inputs * frames // 16, one_rows, 0)

    @pl.when(step == steps - 1)
    def _():
        copy.wait()

        def one_group(group, carry):
            top, rest = high_ref[group], low_ref[group]
            total = jnp.dot(top, table_ref[group, 0], preferred_element_type=jnp.float32)
            total = total + jnp.dot(rest, table_ref[group, 0], preferred_element_type=jnp.float32)
            total = total + jnp.dot(top, table_ref[group, 1], preferred_element_type=jnp.float32)
            spec_ref[group] = total
            return carry

        lax.fori_loop(0, GROUPS, one_group, 0)
        owners = out_ref.shape[0]
        slots = GROUPS
        run = LANES // slots

        def one_part(index, carry):
            first = pl.multiple_of(index * 16, 16)
            slot = lax.broadcasted_iota(jnp.int32, (16, LANES), 1) // run
            picks = [(slot // (1 << bit)) % 2 == 1 for bit in range(3)]
            for kind in range(2):
                for block in range(owners // slots):
                    lanes = pl.ds((kind * (owners // slots) + block) * LANES, LANES)
                    now = [spec_ref[group, pl.ds(first, 16), lanes] for group in range(GROUPS)]
                    for bit in range(3):
                        now = [jnp.where(picks[bit], now[(e - (1 << bit)) % slots], now[e]) for e in range(slots)]
                    for inside in range(slots):
                        out_ref[block * slots + inside, pl.ds(first, 16), pl.ds(kind * LANES, LANES)] = now[inside].astype(jnp.bfloat16)
            return carry

        lax.fori_loop(0, out_ref.shape[1] // 16, one_part, 0)


def filter_bank(samples, history, coefficients, table, first, count, owners):
    _, frames, length = samples.shape
    steps = count // ROWS
    rows = count * frames
    offset = first // ROWS
    return pl.pallas_call(
        functools.partial(filter_bank_kernel, steps),
        out_shape=jax.ShapeDtypeStruct((owners, rows, 2 * LANES), jnp.bfloat16),
        grid=(steps,),
        in_specs=[
            pl.BlockSpec((ROWS, frames, length), lambda i: (i + offset, 0, 0)),
            pl.BlockSpec((ROWS, frames, length), lambda i: (i, 0, 0)),
            pl.BlockSpec(coefficients.shape, lambda i: (0, 0), pipeline_mode=pl.Buffered(1)),
            pl.BlockSpec(memory_space=pl.ANY),
        ],
        out_specs=pl.BlockSpec((owners, rows, 2 * LANES), lambda i: (0, 0, 0), pipeline_mode=pl.Buffered(1)),
        scratch_shapes=[
            pltpu.VMEM((2 * ROWS * frames, LANES), jnp.float32),
            pltpu.VMEM((length // LANES, ROWS * frames, LANES), jnp.float32),
            pltpu.VMEM((GROUPS, rows, 2 * length // RADIX), jnp.bfloat16),
            pltpu.VMEM((GROUPS, rows, 2 * length // RADIX), jnp.bfloat16),
            pltpu.VMEM((GROUPS, rows, 2 * owners * LANES // GROUPS), jnp.float32),
            pltpu.VMEM(table.shape, jnp.bfloat16),
            pltpu.SemaphoreType.DMA,
        ],
        compiler_params=pltpu.CompilerParams(vmem_limit_bytes=56 * MIB),
        cost_estimate=pl.CostEstimate(flops=rows * length * 512 * 3, bytes_accessed=16 * MIB, transcendentals=0),
        name="filter_bank",
    )(samples, history, coefficients, table)


def turn_kernel(frames, in_ref, out_ref, work_ref):
    blocks, rows, _ = in_ref.shape
    count = rows // frames

    def one_input(i, carry):
        first = pl.multiple_of(i * frames, frames)
        pieces = [
            in_ref[t, pl.ds(first, frames), pl.ds(kind * LANES, LANES)]
            for kind in range(2)
            for t in range(blocks)
        ]
        square = jnp.concatenate(pieces, axis=0).astype(jnp.float32)
        work_ref[pl.ds(i, LANES, stride=count), :] = square.T
        return carry

    lax.fori_loop(0, count, one_input, 0)
    out_ref[...] = work_ref[...].reshape(LANES, count, LANES).astype(jnp.bfloat16)


def turn(arrived, sets, frames):
    sources, rows, _ = arrived.shape
    blocks = sources // sets
    count = rows // frames
    return pl.pallas_call(
        functools.partial(turn_kernel, frames),
        out_shape=jax.ShapeDtypeStruct((LANES, sets * count, LANES), jnp.bfloat16),
        grid=(sets,),
        in_specs=[pl.BlockSpec((blocks, rows, 2 * LANES), lambda z: (z, 0, 0))],
        out_specs=pl.BlockSpec((LANES, count, LANES), lambda z: (0, z, 0)),
        scratch_shapes=[pltpu.VMEM((LANES * count, LANES), jnp.float32)],
        compiler_params=pltpu.CompilerParams(vmem_limit_bytes=56 * MIB),
        cost_estimate=pl.CostEstimate(flops=4 * arrived.size, bytes_accessed=4 * arrived.size, transcendentals=0),
        name="turn",
    )(arrived)


def correlate_kernel(counts, sets, scale, order_ref, *refs):
    *in_refs, out_ref = refs
    held = out_ref.shape[0]

    def one_channel(u, carry):
        joined = jnp.concatenate(
            [
                in_ref[u, pl.ds(z * count, count), :]
                for z in range(sets)
                for in_ref, count in zip(in_refs, counts)
            ],
            axis=0,
        )
        lane = lax.broadcasted_iota(jnp.int32, joined.shape, 1)
        wide = pltpu.roll(joined.astype(jnp.float32), LANES // 2, 1)
        turned = jnp.where(lane < LANES // 2, wide, -wide).astype(jnp.bfloat16)
        across = (((1,), (1,)), ((), ()))
        real = lax.dot_general(joined, joined, across, preferred_element_type=jnp.float32)
        imag = lax.dot_general(turned, joined, across, preferred_element_type=jnp.float32)
        row = lax.broadcasted_iota(jnp.int32, real.shape, 0)
        col = lax.broadcasted_iota(jnp.int32, real.shape, 1)
        out_ref[u, 0] = jnp.where(row <= col, real, imag) * scale
        return carry

    lax.fori_loop(0, held, one_channel, 0)


def correlate_all(turned, counts, sets, order, scale):
    channels = turned[0].shape[0]
    held = channels // RADIX
    width = sets * sum(counts)
    out = pl.pallas_call(
        functools.partial(correlate_kernel, counts, sets, scale),
        out_shape=jax.ShapeDtypeStruct((held, RADIX, width, width), jnp.float32),
        grid_spec=pltpu.PrefetchScalarGridSpec(
            num_scalar_prefetch=1,
            grid=(RADIX,),
            in_specs=[pl.BlockSpec((held, sets * count, LANES), lambda s, order: (s, 0, 0)) for count in counts],
            out_specs=pl.BlockSpec((held, 1, width, width), lambda s, order: (0, order[s], 0, 0)),
        ),
        compiler_params=pltpu.CompilerParams(vmem_limit_bytes=56 * MIB),
        cost_estimate=pl.CostEstimate(
            flops=4 * channels * width * width * LANES, bytes_accessed=40 * MIB, transcendentals=0
        ),
        name="correlate",
    )(order, *turned)
    return out.reshape(channels, width, width)


def plan(in_dev):
    return [in_dev // 4] * 4


def fast(samples, coefficients):
    in_dev, frames, length = samples.shape
    everyone = ("inp", "tm", "pol")
    owners = lax.axis_size(everyone)
    sets = lax.axis_size("inp")
    total_frames = frames * owners // sets
    table = jnp.asarray(fourier_tables(length, owners))
    counts = plan(in_dev)
    starts = [sum(counts[:k]) for k in range(len(counts))]
    slot = lax.axis_index(everyone) % GROUPS
    steps = jnp.arange(RADIX, dtype=jnp.int32)
    group, side = (slot - steps // 2) % GROUPS, steps % 2
    order = jnp.where(group == 0, side * GROUPS, jnp.where(side == 0, group, RADIX - group)).astype(jnp.int32)
    turned = []
    for first, count in zip(starts, counts):
        history = from_behind(samples[first : first + count], ("tm", "pol"), 1)
        spectra = filter_bank(samples, history, coefficients, table, first, count, owners)
        arrived = lax.all_to_all(spectra, everyone, 0, 0, tiled=True)
        turned.append(turn(arrived, sets, frames))
    return correlate_all(turned, counts, sets, order, 1.0 / total_frames)


def per_device(samples, coefficients):
    in_dev, frames, length = samples.shape
    taps = coefficients.shape[0]
    owners = lax.axis_size(("inp", "tm", "pol"))
    blocks = lax.axis_size(("tm", "pol"))
    fits = (
        frames == 16
        and taps <= frames + 1
        and in_dev % (4 * ROWS) == 0
        and length == 2 * LANES * owners
        and length % (RADIX * LANES) == 0
        and owners % GROUPS == 0
        and 2 * blocks * frames == LANES
    )
    return fast(samples, coefficients) if fits else general(samples, coefficients)


def solution(mesh):
    placed = (P(("grp", "inp"), ("tm", "pol"), None), P())
    return jax.shard_map(
        per_device,
        mesh=mesh,
        in_specs=placed,
        out_specs=P(("grp", "inp", "tm", "pol"), None, None),
        check_vma=False,
    )
```

```python
import functools
import math

import jax
import jax.numpy as jnp
import ml_dtypes
import numpy as np
from jax import lax
from jax.experimental import pallas as pl
from jax.experimental.pallas import tpu as pltpu
from jax.sharding import PartitionSpec as P

RADIX = 16
GROUPS = RADIX // 2
LANES = 128
ROWS = 8
MIB = 1 << 20


def from_behind(block, axis, distance):
    devices = range(lax.axis_size(axis))
    route = [(i - distance, i) for i in devices if i - distance in devices]
    return lax.ppermute(block, axis, route)


def correlate(real_part, imag_part, total_frames):
    joined = jnp.concatenate([real_part, imag_part], axis=2)
    turned = jnp.concatenate([imag_part, -real_part], axis=2)
    stacked = jnp.concatenate([joined, turned], axis=1)
    product = jnp.einsum("cif,cjf->cij", stacked, joined, preferred_element_type=jnp.float32)
    width = real_part.shape[1]
    row_index = lax.broadcasted_iota(jnp.int32, (width, width), 0)
    col_index = lax.broadcasted_iota(jnp.int32, (width, width), 1)
    packed = jnp.where(row_index <= col_index, product[:, :width], product[:, width:])
    return packed * (1.0 / total_frames)


def filter_frames(block, coefficients, taps):
    frame_count = block.shape[1] - taps + 1
    total = jnp.zeros((block.shape[0], frame_count, block.shape[2]), jnp.float32)
    for tap_index in range(taps):
        total = total + coefficients[tap_index] * block[
            :, tap_index : tap_index + frame_count
        ].astype(jnp.float32)
    return total


def angles(first_idx, second_idx, period):
    product = first_idx[:, None] * second_idx[None, :] % period
    return product.astype(jnp.float32) * (2.0 * math.pi / period)


def transform(filtered):
    row_total, length = filtered.shape
    inner_len = 2 ** ((length.bit_length() - 1) // 2)
    outer_len = length // inner_len
    blocks = filtered.reshape(row_total, inner_len, outer_len)
    inner_idx = jnp.arange(inner_len, dtype=jnp.int32)
    outer_idx = jnp.arange(outer_len, dtype=jnp.int32)
    half_idx = jnp.arange(outer_len // 2, dtype=jnp.int32)
    angle_one = angles(inner_idx, inner_idx, inner_len)
    table_one = jnp.concatenate([jnp.cos(angle_one), -jnp.sin(angle_one)], axis=1)
    section_one = jnp.einsum("rab,ak->rbk", blocks, table_one, precision=lax.Precision.HIGHEST)
    first_re = section_one[..., :inner_len]
    first_im = section_one[..., inner_len:]
    angle_twist = angles(outer_idx, inner_idx, length)
    twist_cos = jnp.cos(angle_twist)
    twist_sin = jnp.sin(angle_twist)
    turned_re = first_re * twist_cos + first_im * twist_sin
    turned_im = first_im * twist_cos - first_re * twist_sin
    angle_two = angles(outer_idx, half_idx, outer_len)
    table_cos = jnp.cos(angle_two)
    table_sin = jnp.sin(angle_two)
    highest = lax.Precision.HIGHEST
    out_re = jnp.einsum("rbk,bq->qkr", turned_re, table_cos, precision=highest) + jnp.einsum(
        "rbk,bq->qkr", turned_im, table_sin, precision=highest
    )
    out_im = jnp.einsum("rbk,bq->qkr", turned_im, table_cos, precision=highest) - jnp.einsum(
        "rbk,bq->qkr", turned_re, table_sin, precision=highest
    )
    scale_factor = 1.0 / math.sqrt(length)
    return jnp.stack([out_re, out_im]).reshape(2, length // 2, row_total) * scale_factor


def general(samples, coefficients):
    in_dev, frame_count, length = samples.shape
    taps = coefficients.shape[0]
    channels = length // 2
    history = from_behind(samples[:, frame_count - taps + 1 :, :], ("tm", "pol"), 1)
    extended = jnp.concatenate([history, samples], axis=1)
    group_size = math.gcd(in_dev, 4)
    spectra_buf = jnp.zeros((2, channels, in_dev, frame_count), jnp.bfloat16)

    def one_group(group_index, buffer_now):
        block = lax.dynamic_slice_in_dim(extended, group_index * group_size, group_size, 0)
        filtered = filter_frames(block, coefficients, taps).reshape(
            group_size * frame_count, length
        )
        spectra_grp = (
            transform(filtered).reshape(2, channels, group_size, frame_count).astype(jnp.bfloat16)
        )
        return lax.dynamic_update_slice_in_dim(buffer_now, spectra_grp, group_index * group_size, 2)

    local_spec = lax.fori_loop(0, in_dev // group_size, one_group, spectra_buf)
    n_inputs = lax.axis_size("inp")
    n_blocks = lax.axis_size("tm")
    n_halves = lax.axis_size("pol")
    total_frames = frame_count * n_blocks * n_halves
    arrived = lax.all_to_all(
        local_spec[None], ("inp", "tm", "pol"), split_axis=2, concat_axis=0, tiled=True
    )
    width = arrived.shape[2]
    arrived = arrived.reshape(n_inputs, n_blocks * n_halves, 2, width, in_dev, frame_count)
    arrived = jnp.transpose(arrived, (2, 3, 0, 4, 1, 5)).reshape(
        2, width, n_inputs * in_dev, n_blocks * n_halves * frame_count
    )
    return correlate(arrived[0], arrived[1], total_frames)


@functools.lru_cache(maxsize=None)
def fourier_tables(length, owners):
    span = length // RADIX
    per_owner = length // 2 // owners // RADIX
    run = 2 * per_owner
    slots = LANES // run
    place = np.arange(span, dtype=np.int64)
    tables = np.zeros((GROUPS, 2 * span, 2 * owners * run))
    for group in range(GROUPS):
        for owner in range(owners):
            block, inside = divmod(owner, slots)
            column = block * LANES + ((inside - group) % slots) * run
            for side in range(2):
                residue = side * GROUPS if group == 0 else (group, RADIX - group)[side]
                channel = RADIX * (owner * per_owner + np.arange(per_owner)) + residue
                angle = 2.0 * np.pi * (place[:, None] * channel[None, :] % length) / length
                cos, sin = np.cos(angle) / math.sqrt(length), np.sin(angle) / math.sqrt(length)
                re = slice(column + side * per_owner, column + (side + 1) * per_owner)
                im = slice(re.start + owners * run, re.stop + owners * run)
                if group == 0:
                    rows = slice(side * span, (side + 1) * span)
                    tables[group, rows, re] = cos
                    tables[group, rows, im] = -sin
                else:
                    sign = 1.0 - 2.0 * side
                    tables[group, :span, re] = cos
                    tables[group, span:, re] = sign * sin
                    tables[group, :span, im] = -sin
                    tables[group, span:, im] = sign * cos
    exact = tables.astype(np.float32)
    high = exact.astype(ml_dtypes.bfloat16)
    low = (exact - high.astype(np.float32)).astype(ml_dtypes.bfloat16)
    return np.stack([high, low], axis=1)


def real_fourier(values):
    count = len(values)
    if count == 1:
        return [(values[0], None)]
    if count == 2:
        return [(values[0] + values[1], None), (values[0] - values[1], None)]
    even, odd = real_fourier(values[0::2]), real_fourier(values[1::2])
    bins = [None] * (count // 2 + 1)
    bins[0] = (even[0][0] + odd[0][0], None)
    bins[count // 2] = (even[0][0] - odd[0][0], None)
    bins[count // 4] = (even[count // 4][0], -odd[count // 4][0])
    for k in range(1, count // 4):
        (er, ei), (pr, pi) = even[k], odd[k]
        if 8 * k == count:
            half = math.sqrt(0.5)
            tr, ti = (pr + pi) * half, (pi - pr) * half
        else:
            c, s = math.cos(2 * math.pi * k / count), math.sin(2 * math.pi * k / count)
            tr, ti = pr * c + pi * s, pi * c - pr * s
        bins[k] = (er + tr, ei + ti)
        bins[count // 2 - k] = (er - tr, ti - ei)
    return bins


def filter_bank_kernel(
    steps, own_ref, old_ref, coef_ref, table_hbm, out_ref, frames_ref, kept_ref, high_ref, low_ref, spec_ref, table_ref, sem
):
    inputs, frames, length = own_ref.shape
    taps = coef_ref.shape[0]
    span = length // RADIX
    parts = span // LANES
    step = pl.program_id(0)
    copy = pltpu.make_async_copy(table_hbm, table_ref, sem)

    @pl.when(step == 0)
    def _():
        copy.start()

    base = step * inputs * frames

    def one_block(block, carry):
        lanes = pl.ds(pl.multiple_of(block * LANES, LANES), LANES)
        for i in range(inputs):
            frames_ref[pl.ds(2 * frames * i, frames), :] = old_ref[i, :, lanes].astype(jnp.float32)
            frames_ref[pl.ds(2 * frames * i + frames, frames), :] = own_ref[i, :, lanes].astype(jnp.float32)
        taps_now = [jnp.broadcast_to(coef_ref[t : t + 1, lanes], (ROWS, LANES)) for t in range(taps)]
        first = frames - taps + 1
        totals = [None] * frames
        for row in range(first, 2 * frames):
            value = frames_ref[pl.ds(row, inputs, stride=2 * frames), :]
            for f in range(max(0, row - first - taps + 1), min(frames, row - first + 1)):
                term = taps_now[row - first - f] * value
                totals[f] = term if totals[f] is None else totals[f] + term
        for f in range(frames):
            kept_ref[block, pl.ds(f, inputs, stride=frames), :] = totals[f]
        return carry

    lax.fori_loop(0, length // LANES, one_block, 0)

    def one_rows(index, carry):
        part = index % parts
        first = pl.multiple_of(index // parts * 16, 16)
        values = [kept_ref[parts * j + part, pl.ds(first, 16), :] for j in range(RADIX)]
        bins = real_fourier(values)
        rows = pl.ds(pl.multiple_of(base + first, 16), 16)
        for group in range(GROUPS):
            pair = (bins[0][0], bins[GROUPS][0]) if group == 0 else bins[group]
            for half in range(2):
                lanes = pl.ds(pl.multiple_of(half * span + part * LANES, LANES), LANES)
                top = pair[half].astype(jnp.bfloat16)
                high_ref[group, rows, lanes] = top
                low_ref[group, rows, lanes] = (pair[half] - top.astype(jnp.float32)).astype(jnp.bfloat16)
        return carry

    lax.fori_loop(0, parts * inputs * frames // 16, one_rows, 0)

    @pl.when(step == steps - 1)
    def _():
        copy.wait()

        def one_group(group, carry):
            top, rest = high_ref[group], low_ref[group]
            total = jnp.dot(top, table_ref[group, 0], preferred_element_type=jnp.float32)
            total = total + jnp.dot(rest, table_ref[group, 0], preferred_element_type=jnp.float32)
            total = total + jnp.dot(top, table_ref[group, 1], preferred_element_type=jnp.float32)
            spec_ref[group] = total
            return carry

        lax.fori_loop(0, GROUPS, one_group, 0, unroll=GROUPS)
        owners = out_ref.shape[0]
        slots = GROUPS
        run = LANES // slots

        def one_part(index, carry):
            first = pl.multiple_of(index * 16, 16)
            slot = lax.broadcasted_iota(jnp.int32, (16, LANES), 1) // run
            picks = [(slot // (1 << bit)) % 2 == 1 for bit in range(3)]
            for kind in range(2):
                for block in range(owners // slots):
                    lanes = pl.ds((kind * (owners // slots) + block) * LANES, LANES)
                    now = [spec_ref[group, pl.ds(first, 16), lanes] for group in range(GROUPS)]
                    for bit in range(3):
                        now = [jnp.where(picks[bit], now[(e - (1 << bit)) % slots], now[e]) for e in range(slots)]
                    for inside in range(slots):
                        out_ref[block * slots + inside, pl.ds(first, 16), pl.ds(kind * LANES, LANES)] = now[inside].astype(jnp.bfloat16)
            return carry

        lax.fori_loop(0, out_ref.shape[1] // 16, one_part, 0)


def filter_bank(samples, history, coefficients, table, first, count, owners):
    _, frames, length = samples.shape
    steps = count // ROWS
    rows = count * frames
    offset = first // ROWS
    return pl.pallas_call(
        functools.partial(filter_bank_kernel, steps),
        out_shape=jax.ShapeDtypeStruct((owners, rows, 2 * LANES), jnp.bfloat16),
        grid=(steps,),
        in_specs=[
            pl.BlockSpec((ROWS, frames, length), lambda i: (i + offset, 0, 0)),
            pl.BlockSpec((ROWS, frames, length), lambda i: (i, 0, 0)),
            pl.BlockSpec(coefficients.shape, lambda i: (0, 0), pipeline_mode=pl.Buffered(1)),
            pl.BlockSpec(memory_space=pl.ANY),
        ],
        out_specs=pl.BlockSpec((owners, rows, 2 * LANES), lambda i: (0, 0, 0), pipeline_mode=pl.Buffered(1)),
        scratch_shapes=[
            pltpu.VMEM((2 * ROWS * frames, LANES), jnp.float32),
            pltpu.VMEM((length // LANES, ROWS * frames, LANES), jnp.float32),
            pltpu.VMEM((GROUPS, rows, 2 * length // RADIX), jnp.bfloat16),
            pltpu.VMEM((GROUPS, rows, 2 * length // RADIX), jnp.bfloat16),
            pltpu.VMEM((GROUPS, rows, 2 * owners * LANES // GROUPS), jnp.float32),
            pltpu.VMEM(table.shape, jnp.bfloat16),
            pltpu.SemaphoreType.DMA,
        ],
        compiler_params=pltpu.CompilerParams(vmem_limit_bytes=56 * MIB),
        cost_estimate=pl.CostEstimate(flops=rows * length * 512 * 3, bytes_accessed=16 * MIB, transcendentals=0),
        name="filter_bank",
    )(samples, history, coefficients, table)


def turn_kernel(frames, in_ref, out_ref, work_ref):
    blocks, rows, _ = in_ref.shape
    count = rows // frames

    def one_input(i, carry):
        first = pl.multiple_of(i * frames, frames)
        pieces = [
            in_ref[t, pl.ds(first, frames), pl.ds(kind * LANES, LANES)]
            for kind in range(2)
            for t in range(blocks)
        ]
        square = jnp.concatenate(pieces, axis=0).astype(jnp.float32)
        work_ref[pl.ds(i, LANES, stride=count), :] = square.T
        return carry

    lax.fori_loop(0, count, one_input, 0, unroll=8)
    out_ref[...] = work_ref[...].reshape(LANES, count, LANES).astype(jnp.bfloat16)


def turn(arrived, sets, frames):
    sources, rows, _ = arrived.shape
    blocks = sources // sets
    count = rows // frames
    return pl.pallas_call(
        functools.partial(turn_kernel, frames),
        out_shape=jax.ShapeDtypeStruct((LANES, sets * count, LANES), jnp.bfloat16),
        grid=(sets,),
        in_specs=[pl.BlockSpec((blocks, rows, 2 * LANES), lambda z: (z, 0, 0))],
        out_specs=pl.BlockSpec((LANES, count, LANES), lambda z: (0, z, 0)),
        scratch_shapes=[pltpu.VMEM((LANES * count, LANES), jnp.float32)],
        compiler_params=pltpu.CompilerParams(vmem_limit_bytes=20 * MIB),
        cost_estimate=pl.CostEstimate(flops=4 * arrived.size, bytes_accessed=4 * arrived.size, transcendentals=0),
        name="turn",
    )(arrived)


def correlate_kernel(counts, sets, scale, order_ref, *refs):
    *in_refs, out_ref = refs
    held = out_ref.shape[0]

    def one_channel(u, carry):
        joined = jnp.concatenate(
            [
                in_ref[u, pl.ds(z * count, count), :]
                for z in range(sets)
                for in_ref, count in zip(in_refs, counts)
            ],
            axis=0,
        )
        turned = jnp.concatenate([joined[:, LANES // 2 :], -joined[:, : LANES // 2]], axis=1)
        both = lax.dot_general(
            jnp.concatenate([joined, turned], axis=0),
            joined,
            (((1,), (1,)), ((), ())),
            preferred_element_type=jnp.float32,
        )
        real, imag = both[: joined.shape[0]], both[joined.shape[0] :]
        row = lax.broadcasted_iota(jnp.int32, real.shape, 0)
        col = lax.broadcasted_iota(jnp.int32, real.shape, 1)
        out_ref[u, 0] = jnp.where(row <= col, real, imag) * scale
        return carry

    lax.fori_loop(0, held, one_channel, 0, unroll=held)


def correlate_all(turned, counts, sets, order, scale):
    channels = turned[0].shape[0]
    held = channels // RADIX
    width = sets * sum(counts)
    out = pl.pallas_call(
        functools.partial(correlate_kernel, counts, sets, scale),
        out_shape=jax.ShapeDtypeStruct((held, RADIX, width, width), jnp.float32),
        grid_spec=pltpu.PrefetchScalarGridSpec(
            num_scalar_prefetch=1,
            grid=(RADIX,),
            in_specs=[pl.BlockSpec((held, sets * count, LANES), lambda s, order: (s, 0, 0)) for count in counts],
            out_specs=pl.BlockSpec((held, 1, width, width), lambda s, order: (0, order[s], 0, 0)),
        ),
        compiler_params=pltpu.CompilerParams(vmem_limit_bytes=24 * MIB),
        cost_estimate=pl.CostEstimate(
            flops=4 * channels * width * width * LANES, bytes_accessed=40 * MIB, transcendentals=0
        ),
        name="correlate",
    )(order, *turned)
    return out.reshape(channels, width, width)


def plan(in_dev):
    return [in_dev // 4] * 4


def fast(samples, coefficients):
    in_dev, frames, length = samples.shape
    everyone = ("inp", "tm", "pol")
    owners = lax.axis_size(everyone)
    sets = lax.axis_size("inp")
    total_frames = frames * owners // sets
    table = jnp.asarray(fourier_tables(length, owners))
    counts = plan(in_dev)
    starts = [sum(counts[:k]) for k in range(len(counts))]
    slot = lax.axis_index(everyone) % GROUPS
    steps = jnp.arange(RADIX, dtype=jnp.int32)
    group, side = (slot - steps // 2) % GROUPS, steps % 2
    order = jnp.where(group == 0, side * GROUPS, jnp.where(side == 0, group, RADIX - group)).astype(jnp.int32)
    histories, source = [], samples
    for first, count in zip(starts, counts):
        histories.append(from_behind(source[first : first + count], ("tm", "pol"), 1))
        source, histories[-1] = lax.optimization_barrier((source, histories[-1]))
    turned = []
    for k, (first, count) in enumerate(zip(starts, counts)):
        spectra = filter_bank(samples, histories[k], coefficients, table, first, count, owners)
        if k + 1 < len(counts):
            spectra, histories[k + 1] = lax.optimization_barrier((spectra, histories[k + 1]))
        arrived = lax.all_to_all(spectra, everyone, 0, 0, tiled=True)
        turned.append(turn(arrived, sets, frames))
    return correlate_all(turned, counts, sets, order, 1.0 / total_frames)


def per_device(samples, coefficients):
    in_dev, frames, length = samples.shape
    taps = coefficients.shape[0]
    owners = lax.axis_size(("inp", "tm", "pol"))
    blocks = lax.axis_size(("tm", "pol"))
    fits = (
        frames == 16
        and taps <= frames + 1
        and in_dev % (4 * ROWS) == 0
        and length == 2 * LANES * owners
        and length % (RADIX * LANES) == 0
        and owners % GROUPS == 0
        and 2 * blocks * frames == LANES
    )
    return fast(samples, coefficients) if fits else general(samples, coefficients)


def solution(mesh):
    placed = (P(("grp", "inp"), ("tm", "pol"), None), P())
    return jax.shard_map(
        per_device,
        mesh=mesh,
        in_specs=placed,
        out_specs=P(("grp", "inp", "tm", "pol"), None, None),
        check_vma=False,
    )
```

```python
import functools
import math

import jax
import jax.numpy as jnp
import ml_dtypes
import numpy as np
from jax import lax
from jax.experimental import pallas as pl
from jax.experimental.pallas import tpu as pltpu
from jax.sharding import PartitionSpec as P

RADIX = 16
GROUPS = RADIX // 2
LANES = 128
ROWS = 8
MIB = 1 << 20


def from_behind(block, axis, distance):
    devices = range(lax.axis_size(axis))
    route = [(i - distance, i) for i in devices if i - distance in devices]
    return lax.ppermute(block, axis, route)


def correlate(real_part, imag_part, total_frames):
    joined = jnp.concatenate([real_part, imag_part], axis=2)
    turned = jnp.concatenate([imag_part, -real_part], axis=2)
    stacked = jnp.concatenate([joined, turned], axis=1)
    product = jnp.einsum("cif,cjf->cij", stacked, joined, preferred_element_type=jnp.float32)
    width = real_part.shape[1]
    row_index = lax.broadcasted_iota(jnp.int32, (width, width), 0)
    col_index = lax.broadcasted_iota(jnp.int32, (width, width), 1)
    packed = jnp.where(row_index <= col_index, product[:, :width], product[:, width:])
    return packed * (1.0 / total_frames)


def filter_frames(block, coefficients, taps):
    frame_count = block.shape[1] - taps + 1
    total = jnp.zeros((block.shape[0], frame_count, block.shape[2]), jnp.float32)
    for tap_index in range(taps):
        total = total + coefficients[tap_index] * block[
            :, tap_index : tap_index + frame_count
        ].astype(jnp.float32)
    return total


def angles(first_idx, second_idx, period):
    product = first_idx[:, None] * second_idx[None, :] % period
    return product.astype(jnp.float32) * (2.0 * math.pi / period)


def transform(filtered):
    row_total, length = filtered.shape
    inner_len = 2 ** ((length.bit_length() - 1) // 2)
    outer_len = length // inner_len
    blocks = filtered.reshape(row_total, inner_len, outer_len)
    inner_idx = jnp.arange(inner_len, dtype=jnp.int32)
    outer_idx = jnp.arange(outer_len, dtype=jnp.int32)
    half_idx = jnp.arange(outer_len // 2, dtype=jnp.int32)
    angle_one = angles(inner_idx, inner_idx, inner_len)
    table_one = jnp.concatenate([jnp.cos(angle_one), -jnp.sin(angle_one)], axis=1)
    section_one = jnp.einsum("rab,ak->rbk", blocks, table_one, precision=lax.Precision.HIGHEST)
    first_re = section_one[..., :inner_len]
    first_im = section_one[..., inner_len:]
    angle_twist = angles(outer_idx, inner_idx, length)
    twist_cos = jnp.cos(angle_twist)
    twist_sin = jnp.sin(angle_twist)
    turned_re = first_re * twist_cos + first_im * twist_sin
    turned_im = first_im * twist_cos - first_re * twist_sin
    angle_two = angles(outer_idx, half_idx, outer_len)
    table_cos = jnp.cos(angle_two)
    table_sin = jnp.sin(angle_two)
    highest = lax.Precision.HIGHEST
    out_re = jnp.einsum("rbk,bq->qkr", turned_re, table_cos, precision=highest) + jnp.einsum(
        "rbk,bq->qkr", turned_im, table_sin, precision=highest
    )
    out_im = jnp.einsum("rbk,bq->qkr", turned_im, table_cos, precision=highest) - jnp.einsum(
        "rbk,bq->qkr", turned_re, table_sin, precision=highest
    )
    scale_factor = 1.0 / math.sqrt(length)
    return jnp.stack([out_re, out_im]).reshape(2, length // 2, row_total) * scale_factor


def general(samples, coefficients):
    in_dev, frame_count, length = samples.shape
    taps = coefficients.shape[0]
    channels = length // 2
    history = from_behind(samples[:, frame_count - taps + 1 :, :], ("tm", "pol"), 1)
    extended = jnp.concatenate([history, samples], axis=1)
    group_size = math.gcd(in_dev, 4)
    spectra_buf = jnp.zeros((2, channels, in_dev, frame_count), jnp.bfloat16)

    def one_group(group_index, buffer_now):
        block = lax.dynamic_slice_in_dim(extended, group_index * group_size, group_size, 0)
        filtered = filter_frames(block, coefficients, taps).reshape(
            group_size * frame_count, length
        )
        spectra_grp = (
            transform(filtered).reshape(2, channels, group_size, frame_count).astype(jnp.bfloat16)
        )
        return lax.dynamic_update_slice_in_dim(buffer_now, spectra_grp, group_index * group_size, 2)

    local_spec = lax.fori_loop(0, in_dev // group_size, one_group, spectra_buf)
    n_inputs = lax.axis_size("inp")
    n_blocks = lax.axis_size("tm")
    n_halves = lax.axis_size("pol")
    total_frames = frame_count * n_blocks * n_halves
    arrived = lax.all_to_all(
        local_spec[None], ("inp", "tm", "pol"), split_axis=2, concat_axis=0, tiled=True
    )
    width = arrived.shape[2]
    arrived = arrived.reshape(n_inputs, n_blocks * n_halves, 2, width, in_dev, frame_count)
    arrived = jnp.transpose(arrived, (2, 3, 0, 4, 1, 5)).reshape(
        2, width, n_inputs * in_dev, n_blocks * n_halves * frame_count
    )
    return correlate(arrived[0], arrived[1], total_frames)


@functools.lru_cache(maxsize=None)
def fourier_tables(length, owners):
    span = length // RADIX
    per_owner = length // 2 // owners // RADIX
    run = 2 * per_owner
    slots = LANES // run
    place = np.arange(span, dtype=np.int64)
    tables = np.zeros((GROUPS, 2 * span, 2 * owners * run))
    for group in range(GROUPS):
        for owner in range(owners):
            block, inside = divmod(owner, slots)
            column = block * LANES + ((inside - group) % slots) * run
            for side in range(2):
                residue = side * GROUPS if group == 0 else (group, RADIX - group)[side]
                channel = RADIX * (owner * per_owner + np.arange(per_owner)) + residue
                angle = 2.0 * np.pi * (place[:, None] * channel[None, :] % length) / length
                cos, sin = np.cos(angle) / math.sqrt(length), np.sin(angle) / math.sqrt(length)
                re = slice(column + side * per_owner, column + (side + 1) * per_owner)
                im = slice(re.start + owners * run, re.stop + owners * run)
                if group == 0:
                    rows = slice(side * span, (side + 1) * span)
                    tables[group, rows, re] = cos
                    tables[group, rows, im] = -sin
                else:
                    sign = 1.0 - 2.0 * side
                    tables[group, :span, re] = cos
                    tables[group, span:, re] = sign * sin
                    tables[group, :span, im] = -sin
                    tables[group, span:, im] = sign * cos
    exact = tables.astype(np.float32)
    high = exact.astype(ml_dtypes.bfloat16)
    low = (exact - high.astype(np.float32)).astype(ml_dtypes.bfloat16)
    return np.stack([high, low], axis=1)


def real_fourier(values):
    count = len(values)
    if count == 1:
        return [(values[0], None)]
    if count == 2:
        return [(values[0] + values[1], None), (values[0] - values[1], None)]
    even, odd = real_fourier(values[0::2]), real_fourier(values[1::2])
    bins = [None] * (count // 2 + 1)
    bins[0] = (even[0][0] + odd[0][0], None)
    bins[count // 2] = (even[0][0] - odd[0][0], None)
    bins[count // 4] = (even[count // 4][0], -odd[count // 4][0])
    for k in range(1, count // 4):
        (er, ei), (pr, pi) = even[k], odd[k]
        if 8 * k == count:
            half = math.sqrt(0.5)
            tr, ti = (pr + pi) * half, (pi - pr) * half
        else:
            c, s = math.cos(2 * math.pi * k / count), math.sin(2 * math.pi * k / count)
            tr, ti = pr * c + pi * s, pi * c - pr * s
        bins[k] = (er + tr, ei + ti)
        bins[count // 2 - k] = (er - tr, ti - ei)
    return bins


def filter_bank_kernel(steps, following, own_ref, coef_ref, table_hbm, history_hbm, *refs):
    if following:
        samples_hbm, out_ref, piece_hbm, *refs, piece_ref = refs
        fetch = pltpu.make_async_copy(samples_hbm.at[pl.ds(*following)], piece_ref, refs[-1].at[steps + 1])
        store = pltpu.make_async_copy(piece_ref, piece_hbm, refs[-1].at[steps + 2])
    else:
        out_ref, *refs = refs
    past_ref, frames_ref, kept_ref, high_ref, low_ref, spec_ref, table_ref, sems = refs
    inputs, frames, length = own_ref.shape
    taps = coef_ref.shape[0]
    span = length // RADIX
    parts = span // LANES
    step = pl.program_id(0)
    copy = pltpu.make_async_copy(table_hbm, table_ref, sems.at[steps])

    @pl.when(step == 0)
    def _():
        for k in range(steps):
            pltpu.make_async_copy(history_hbm.at[pl.ds(k * inputs, inputs)], past_ref.at[k], sems.at[k]).start()
        copy.start()
        if following:
            fetch.start()

    for k in range(steps):

        @pl.when(step == k)
        def _():
            pltpu.make_async_copy(history_hbm.at[pl.ds(k * inputs, inputs)], past_ref.at[k], sems.at[k]).wait()

    base = step * inputs * frames

    def one_block(block, carry):
        lanes = pl.ds(pl.multiple_of(block * LANES, LANES), LANES)
        for i in range(inputs):
            frames_ref[pl.ds(2 * frames * i, frames), :] = past_ref[step, i, :, lanes].astype(jnp.float32)
            frames_ref[pl.ds(2 * frames * i + frames, frames), :] = own_ref[i, :, lanes].astype(jnp.float32)
        taps_now = [jnp.broadcast_to(coef_ref[t : t + 1, lanes], (ROWS, LANES)) for t in range(taps)]
        first = frames - taps + 1
        totals = [None] * frames
        for row in range(first, 2 * frames):
            value = frames_ref[pl.ds(row, inputs, stride=2 * frames), :]
            for f in range(max(0, row - first - taps + 1), min(frames, row - first + 1)):
                term = taps_now[row - first - f] * value
                totals[f] = term if totals[f] is None else totals[f] + term
        for f in range(frames):
            kept_ref[block, pl.ds(f, inputs, stride=frames), :] = totals[f]
        return carry

    lax.fori_loop(0, length // LANES, one_block, 0)
    if following:

        @pl.when(step == 0)
        def _():
            fetch.wait()
            store.start()


    def one_rows(index, carry):
        part = index % parts
        first = pl.multiple_of(index // parts * 16, 16)
        values = [kept_ref[parts * j + part, pl.ds(first, 16), :] for j in range(RADIX)]
        bins = real_fourier(values)
        rows = pl.ds(pl.multiple_of(base + first, 16), 16)
        for group in range(GROUPS):
            pair = (bins[0][0], bins[GROUPS][0]) if group == 0 else bins[group]
            for half in range(2):
                lanes = pl.ds(pl.multiple_of(half * span + part * LANES, LANES), LANES)
                top = pair[half].astype(jnp.bfloat16)
                high_ref[group, rows, lanes] = top
                low_ref[group, rows, lanes] = (pair[half] - top.astype(jnp.float32)).astype(jnp.bfloat16)
        return carry

    lax.fori_loop(0, parts * inputs * frames // 16, one_rows, 0)

    @pl.when(step == steps - 1)
    def _():
        copy.wait()

        def one_group(group, carry):
            top, rest = high_ref[group], low_ref[group]
            total = jnp.dot(top, table_ref[group, 0], preferred_element_type=jnp.float32)
            total = total + jnp.dot(rest, table_ref[group, 0], preferred_element_type=jnp.float32)
            total = total + jnp.dot(top, table_ref[group, 1], preferred_element_type=jnp.float32)
            spec_ref[group] = total
            return carry

        lax.fori_loop(0, GROUPS, one_group, 0, unroll=GROUPS)
        owners = out_ref.shape[0]
        slots = GROUPS
        run = LANES // slots

        def one_part(index, carry):
            first = pl.multiple_of(index * 16, 16)
            slot = lax.broadcasted_iota(jnp.int32, (16, LANES), 1) // run
            picks = [(slot // (1 << bit)) % 2 == 1 for bit in range(3)]
            for kind in range(2):
                for block in range(owners // slots):
                    lanes = pl.ds((kind * (owners // slots) + block) * LANES, LANES)
                    now = [spec_ref[group, pl.ds(first, 16), lanes] for group in range(GROUPS)]
                    for bit in range(3):
                        now = [jnp.where(picks[bit], now[(e - (1 << bit)) % slots], now[e]) for e in range(slots)]
                    for inside in range(slots):
                        out_ref[block * slots + inside, pl.ds(first, 16), pl.ds(kind * LANES, LANES)] = now[inside].astype(jnp.bfloat16)
            return carry

        lax.fori_loop(0, out_ref.shape[1] // 16, one_part, 0)
        if following:
            store.wait()


def filter_bank(samples, history, coefficients, table, first, count, owners, following):
    _, frames, length = samples.shape
    steps = count // ROWS
    rows = count * frames
    offset = first // ROWS
    in_specs = [
        pl.BlockSpec((ROWS, frames, length), lambda i: (i + offset, 0, 0)),
        pl.BlockSpec(coefficients.shape, lambda i: (0, 0), pipeline_mode=pl.Buffered(1)),
        pl.BlockSpec(memory_space=pl.ANY),
        pl.BlockSpec(memory_space=pl.ANY),
    ]
    out_specs = [pl.BlockSpec((owners, rows, 2 * LANES), lambda i: (0, 0, 0), pipeline_mode=pl.Buffered(1))]
    out_shape = [jax.ShapeDtypeStruct((owners, rows, 2 * LANES), jnp.bfloat16)]
    operands = [samples, coefficients, table, history]
    if following:
        in_specs.append(pl.BlockSpec(memory_space=pl.ANY))
        out_specs.append(pl.BlockSpec(memory_space=pl.ANY))
        out_shape.append(jax.ShapeDtypeStruct((following[1], frames, length), samples.dtype))
        operands.append(samples)
    return pl.pallas_call(
        functools.partial(filter_bank_kernel, steps, following),
        out_shape=out_shape,
        grid=(steps,),
        in_specs=in_specs,
        out_specs=out_specs,
        scratch_shapes=[
            pltpu.VMEM((steps, ROWS, frames, length), jnp.bfloat16),
            pltpu.VMEM((2 * ROWS * frames, LANES), jnp.float32),
            pltpu.VMEM((length // LANES, ROWS * frames, LANES), jnp.float32),
            pltpu.VMEM((GROUPS, rows, 2 * length // RADIX), jnp.bfloat16),
            pltpu.VMEM((GROUPS, rows, 2 * length // RADIX), jnp.bfloat16),
            pltpu.VMEM((GROUPS, rows, 2 * owners * LANES // GROUPS), jnp.float32),
            pltpu.VMEM(table.shape, jnp.bfloat16),
            pltpu.SemaphoreType.DMA((steps + 3,)),
        ]
        + ([pltpu.VMEM((following[1], frames, length), samples.dtype)] if following else []),
        compiler_params=pltpu.CompilerParams(vmem_limit_bytes=62 * MIB),
        cost_estimate=pl.CostEstimate(flops=10**11, bytes_accessed=16 * MIB, transcendentals=0),
        name="filter_bank",
    )(*operands)


def cut_kernel(in_ref, out_ref):
    out_ref[...] = in_ref[...]


def cut(samples, first, count):
    block = (ROWS, *samples.shape[1:])
    return pl.pallas_call(
        cut_kernel,
        out_shape=jax.ShapeDtypeStruct((count, *samples.shape[1:]), samples.dtype),
        grid=(count // ROWS,),
        in_specs=[pl.BlockSpec(block, lambda i: (i + first // ROWS, 0, 0))],
        out_specs=pl.BlockSpec(block, lambda i: (i, 0, 0)),
        cost_estimate=pl.CostEstimate(flops=0, bytes_accessed=4 * MIB, transcendentals=0),
        name="cut",
    )(samples)


def turn_kernel(frames, in_ref, out_ref, work_ref):
    blocks, rows, _ = in_ref.shape
    count = rows // frames

    def one_input(i, carry):
        first = pl.multiple_of(i * frames, frames)
        pieces = [
            in_ref[t, pl.ds(first, frames), pl.ds(kind * LANES, LANES)]
            for kind in range(2)
            for t in range(blocks)
        ]
        square = jnp.concatenate(pieces, axis=0).astype(jnp.float32)
        work_ref[pl.ds(i, LANES, stride=count), :] = square.T
        return carry

    lax.fori_loop(0, count, one_input, 0, unroll=8)
    out_ref[...] = work_ref[...].reshape(LANES, count, LANES).astype(jnp.bfloat16)


def turn(arrived, sets, frames):
    sources, rows, _ = arrived.shape
    blocks = sources // sets
    count = rows // frames
    return pl.pallas_call(
        functools.partial(turn_kernel, frames),
        out_shape=jax.ShapeDtypeStruct((LANES, sets * count, LANES), jnp.bfloat16),
        grid=(sets,),
        in_specs=[pl.BlockSpec((blocks, rows, 2 * LANES), lambda z: (z, 0, 0))],
        out_specs=pl.BlockSpec((LANES, count, LANES), lambda z: (0, z, 0)),
        scratch_shapes=[pltpu.VMEM((LANES * count, LANES), jnp.float32)],
        compiler_params=pltpu.CompilerParams(vmem_limit_bytes=20 * MIB),
        cost_estimate=pl.CostEstimate(flops=4 * arrived.size, bytes_accessed=4 * arrived.size, transcendentals=0),
        name="turn",
    )(arrived)


def correlate_kernel(counts, sets, scale, order_ref, *refs):
    *in_refs, out_ref = refs
    held = out_ref.shape[0]

    def one_channel(u, carry):
        joined = jnp.concatenate(
            [
                in_ref[u, pl.ds(z * count, count), :]
                for z in range(sets)
                for in_ref, count in zip(in_refs, counts)
            ],
            axis=0,
        )
        turned = jnp.concatenate([joined[:, LANES // 2 :], -joined[:, : LANES // 2]], axis=1)
        both = lax.dot_general(
            jnp.concatenate([joined, turned], axis=0),
            joined,
            (((1,), (1,)), ((), ())),
            preferred_element_type=jnp.float32,
        )
        real, imag = both[: joined.shape[0]], both[joined.shape[0] :]
        row = lax.broadcasted_iota(jnp.int32, real.shape, 0)
        col = lax.broadcasted_iota(jnp.int32, real.shape, 1)
        out_ref[u, 0] = jnp.where(row <= col, real, imag) * scale
        return carry

    lax.fori_loop(0, held, one_channel, 0, unroll=held)


def correlate_all(turned, counts, sets, order, scale):
    channels = turned[0].shape[0]
    held = channels // RADIX
    width = sets * sum(counts)
    out = pl.pallas_call(
        functools.partial(correlate_kernel, counts, sets, scale),
        out_shape=jax.ShapeDtypeStruct((held, RADIX, width, width), jnp.float32),
        grid_spec=pltpu.PrefetchScalarGridSpec(
            num_scalar_prefetch=1,
            grid=(RADIX,),
            in_specs=[pl.BlockSpec((held, sets * count, LANES), lambda s, order: (s, 0, 0)) for count in counts],
            out_specs=pl.BlockSpec((held, 1, width, width), lambda s, order: (0, order[s], 0, 0)),
        ),
        compiler_params=pltpu.CompilerParams(vmem_limit_bytes=24 * MIB),
        cost_estimate=pl.CostEstimate(
            flops=4 * channels * width * width * LANES, bytes_accessed=40 * MIB, transcendentals=0
        ),
        name="correlate",
    )(order, *turned)
    return out.reshape(channels, width, width)


def plan(in_dev):
    units = in_dev // ROWS
    return [ROWS * size for size in (1, 2, 2, units - 5)]


def fast(samples, coefficients):
    in_dev, frames, length = samples.shape
    everyone = ("inp", "tm", "pol")
    owners = lax.axis_size(everyone)
    sets = lax.axis_size("inp")
    total_frames = frames * owners // sets
    table = jnp.asarray(fourier_tables(length, owners))
    counts = plan(in_dev)
    starts = [sum(counts[:k]) for k in range(len(counts))]
    slot = lax.axis_index(everyone) % GROUPS
    steps = jnp.arange(RADIX, dtype=jnp.int32)
    group, side = (slot - steps // 2) % GROUPS, steps % 2
    order = jnp.where(group == 0, side * GROUPS, jnp.where(side == 0, group, RADIX - group)).astype(jnp.int32)
    last = len(counts) - 1
    parts = list(zip(starts, counts))
    histories = [from_behind(samples[: counts[0]], ("tm", "pol"), 1)]
    piece, histories[0] = lax.optimization_barrier((cut(samples, *parts[1]), histories[0]))
    histories.append(from_behind(piece, ("tm", "pol"), 1))
    turned = []
    for k in range(last + 1):
        following = parts[k + 2] if k + 2 <= last else None
        spectra, *pieces = filter_bank(
            samples, histories[k], coefficients, table, starts[k], counts[k], owners, following
        )
        if following:
            piece = pieces[0]
            if k > 0:
                piece, arrived = lax.optimization_barrier((piece, arrived))
            piece, histories[k + 1] = lax.optimization_barrier((piece, histories[k + 1]))
            histories.append(from_behind(piece, ("tm", "pol"), 1))
        if k > 0:
            turned.append(turn(arrived, sets, frames))
        arrived = lax.all_to_all(spectra, everyone, 0, 0, tiled=True)
    turned.append(turn(arrived, sets, frames))
    return correlate_all(turned, counts, sets, order, 1.0 / total_frames)


def per_device(samples, coefficients):
    in_dev, frames, length = samples.shape
    taps = coefficients.shape[0]
    owners = lax.axis_size(("inp", "tm", "pol"))
    blocks = lax.axis_size(("tm", "pol"))
    fits = (
        frames == 16
        and taps <= frames + 1
        and in_dev % (4 * ROWS) == 0
        and length == 2 * LANES * owners
        and length % (RADIX * LANES) == 0
        and owners % GROUPS == 0
        and 2 * blocks * frames == LANES
    )
    return fast(samples, coefficients) if fits else general(samples, coefficients)


def solution(mesh):
    placed = (P(("grp", "inp"), ("tm", "pol"), None), P())
    return jax.shard_map(
        per_device,
        mesh=mesh,
        in_specs=placed,
        out_specs=P(("grp", "inp", "tm", "pol"), None, None),
        check_vma=False,
    )
```

```python
import functools
import math

import jax
import jax.numpy as jnp
import ml_dtypes
import numpy as np
from jax import lax
from jax.experimental import pallas as pl
from jax.experimental.pallas import tpu as pltpu
from jax.sharding import PartitionSpec as P

RADIX = 16
GROUPS = RADIX // 2
LANES = 128
ROWS = 8
MIB = 1 << 20


def from_behind(block, axis, distance):
    devices = range(lax.axis_size(axis))
    route = [(i - distance, i) for i in devices if i - distance in devices]
    return lax.ppermute(block, axis, route)


def correlate(real_part, imag_part, total_frames):
    joined = jnp.concatenate([real_part, imag_part], axis=2)
    turned = jnp.concatenate([imag_part, -real_part], axis=2)
    stacked = jnp.concatenate([joined, turned], axis=1)
    product = jnp.einsum("cif,cjf->cij", stacked, joined, preferred_element_type=jnp.float32)
    width = real_part.shape[1]
    row_index = lax.broadcasted_iota(jnp.int32, (width, width), 0)
    col_index = lax.broadcasted_iota(jnp.int32, (width, width), 1)
    packed = jnp.where(row_index <= col_index, product[:, :width], product[:, width:])
    return packed * (1.0 / total_frames)


def filter_frames(block, coefficients, taps):
    frame_count = block.shape[1] - taps + 1
    total = jnp.zeros((block.shape[0], frame_count, block.shape[2]), jnp.float32)
    for tap_index in range(taps):
        total = total + coefficients[tap_index] * block[
            :, tap_index : tap_index + frame_count
        ].astype(jnp.float32)
    return total


def angles(first_idx, second_idx, period):
    product = first_idx[:, None] * second_idx[None, :] % period
    return product.astype(jnp.float32) * (2.0 * math.pi / period)


def transform(filtered):
    row_total, length = filtered.shape
    inner_len = 2 ** ((length.bit_length() - 1) // 2)
    outer_len = length // inner_len
    blocks = filtered.reshape(row_total, inner_len, outer_len)
    inner_idx = jnp.arange(inner_len, dtype=jnp.int32)
    outer_idx = jnp.arange(outer_len, dtype=jnp.int32)
    half_idx = jnp.arange(outer_len // 2, dtype=jnp.int32)
    angle_one = angles(inner_idx, inner_idx, inner_len)
    table_one = jnp.concatenate([jnp.cos(angle_one), -jnp.sin(angle_one)], axis=1)
    section_one = jnp.einsum("rab,ak->rbk", blocks, table_one, precision=lax.Precision.HIGHEST)
    first_re = section_one[..., :inner_len]
    first_im = section_one[..., inner_len:]
    angle_twist = angles(outer_idx, inner_idx, length)
    twist_cos = jnp.cos(angle_twist)
    twist_sin = jnp.sin(angle_twist)
    turned_re = first_re * twist_cos + first_im * twist_sin
    turned_im = first_im * twist_cos - first_re * twist_sin
    angle_two = angles(outer_idx, half_idx, outer_len)
    table_cos = jnp.cos(angle_two)
    table_sin = jnp.sin(angle_two)
    highest = lax.Precision.HIGHEST
    out_re = jnp.einsum("rbk,bq->qkr", turned_re, table_cos, precision=highest) + jnp.einsum(
        "rbk,bq->qkr", turned_im, table_sin, precision=highest
    )
    out_im = jnp.einsum("rbk,bq->qkr", turned_im, table_cos, precision=highest) - jnp.einsum(
        "rbk,bq->qkr", turned_re, table_sin, precision=highest
    )
    scale_factor = 1.0 / math.sqrt(length)
    return jnp.stack([out_re, out_im]).reshape(2, length // 2, row_total) * scale_factor


def general(samples, coefficients):
    in_dev, frame_count, length = samples.shape
    taps = coefficients.shape[0]
    channels = length // 2
    history = from_behind(samples[:, frame_count - taps + 1 :, :], ("tm", "pol"), 1)
    extended = jnp.concatenate([history, samples], axis=1)
    group_size = math.gcd(in_dev, 4)
    spectra_buf = jnp.zeros((2, channels, in_dev, frame_count), jnp.bfloat16)

    def one_group(group_index, buffer_now):
        block = lax.dynamic_slice_in_dim(extended, group_index * group_size, group_size, 0)
        filtered = filter_frames(block, coefficients, taps).reshape(
            group_size * frame_count, length
        )
        spectra_grp = (
            transform(filtered).reshape(2, channels, group_size, frame_count).astype(jnp.bfloat16)
        )
        return lax.dynamic_update_slice_in_dim(buffer_now, spectra_grp, group_index * group_size, 2)

    local_spec = lax.fori_loop(0, in_dev // group_size, one_group, spectra_buf)
    n_inputs = lax.axis_size("inp")
    n_blocks = lax.axis_size("tm")
    n_halves = lax.axis_size("pol")
    total_frames = frame_count * n_blocks * n_halves
    arrived = lax.all_to_all(
        local_spec[None], ("inp", "tm", "pol"), split_axis=2, concat_axis=0, tiled=True
    )
    width = arrived.shape[2]
    arrived = arrived.reshape(n_inputs, n_blocks * n_halves, 2, width, in_dev, frame_count)
    arrived = jnp.transpose(arrived, (2, 3, 0, 4, 1, 5)).reshape(
        2, width, n_inputs * in_dev, n_blocks * n_halves * frame_count
    )
    return correlate(arrived[0], arrived[1], total_frames)


@functools.lru_cache(maxsize=None)
def fourier_tables(length, owners):
    span = length // RADIX
    per_owner = length // 2 // owners // RADIX
    run = 2 * per_owner
    slots = LANES // run
    place = np.arange(span, dtype=np.int64)
    tables = np.zeros((GROUPS, 2 * span, 2 * owners * run))
    for group in range(GROUPS):
        for owner in range(owners):
            block, inside = divmod(owner, slots)
            column = block * LANES + ((inside - group) % slots) * run
            for side in range(2):
                residue = side * GROUPS if group == 0 else (group, RADIX - group)[side]
                channel = RADIX * (owner * per_owner + np.arange(per_owner)) + residue
                angle = 2.0 * np.pi * (place[:, None] * channel[None, :] % length) / length
                cos, sin = np.cos(angle) / math.sqrt(length), np.sin(angle) / math.sqrt(length)
                re = slice(column + side * per_owner, column + (side + 1) * per_owner)
                im = slice(re.start + owners * run, re.stop + owners * run)
                if group == 0:
                    rows = slice(side * span, (side + 1) * span)
                    tables[group, rows, re] = cos
                    tables[group, rows, im] = -sin
                else:
                    sign = 1.0 - 2.0 * side
                    tables[group, :span, re] = cos
                    tables[group, span:, re] = sign * sin
                    tables[group, :span, im] = -sin
                    tables[group, span:, im] = sign * cos
    exact = tables.astype(np.float32)
    high = exact.astype(ml_dtypes.bfloat16)
    low = (exact - high.astype(np.float32)).astype(ml_dtypes.bfloat16)
    return np.stack([high, low], axis=1)


def real_fourier(values):
    count = len(values)
    if count == 1:
        return [(values[0], None)]
    if count == 2:
        return [(values[0] + values[1], None), (values[0] - values[1], None)]
    even, odd = real_fourier(values[0::2]), real_fourier(values[1::2])
    bins = [None] * (count // 2 + 1)
    bins[0] = (even[0][0] + odd[0][0], None)
    bins[count // 2] = (even[0][0] - odd[0][0], None)
    bins[count // 4] = (even[count // 4][0], -odd[count // 4][0])
    for k in range(1, count // 4):
        (er, ei), (pr, pi) = even[k], odd[k]
        if 8 * k == count:
            half = math.sqrt(0.5)
            tr, ti = (pr + pi) * half, (pi - pr) * half
        else:
            c, s = math.cos(2 * math.pi * k / count), math.sin(2 * math.pi * k / count)
            tr, ti = pr * c + pi * s, pi * c - pr * s
        bins[k] = (er + tr, ei + ti)
        bins[count // 2 - k] = (er - tr, ti - ei)
    return bins


def filter_bank_kernel(steps, following, own_ref, coef_ref, table_hbm, history_hbm, *refs):
    if following:
        samples_hbm, out_ref, piece_hbm, *refs, piece_ref = refs
        fetch = pltpu.make_async_copy(samples_hbm.at[pl.ds(*following)], piece_ref, refs[-1].at[steps + 1])
        store = pltpu.make_async_copy(piece_ref, piece_hbm, refs[-1].at[steps + 2])
    else:
        out_ref, *refs = refs
    past_ref, frames_ref, kept_ref, high_ref, low_ref, spec_ref, table_ref, sems = refs
    inputs, frames, length = own_ref.shape
    taps = coef_ref.shape[0]
    span = length // RADIX
    parts = span // LANES
    step = pl.program_id(0)
    copy = pltpu.make_async_copy(table_hbm, table_ref, sems.at[steps])

    @pl.when(step == 0)
    def _():
        for k in range(steps):
            pltpu.make_async_copy(history_hbm.at[pl.ds(k * inputs, inputs)], past_ref.at[k], sems.at[k]).start()
        copy.start()
        if following:
            fetch.start()

    for k in range(steps):

        @pl.when(step == k)
        def _():
            pltpu.make_async_copy(history_hbm.at[pl.ds(k * inputs, inputs)], past_ref.at[k], sems.at[k]).wait()

    base = step * inputs * frames

    def one_block(block, carry):
        lanes = pl.ds(pl.multiple_of(block * LANES, LANES), LANES)
        for i in range(inputs):
            frames_ref[pl.ds(2 * frames * i, frames), :] = past_ref[step, i, :, lanes].astype(jnp.float32)
            frames_ref[pl.ds(2 * frames * i + frames, frames), :] = own_ref[i, :, lanes].astype(jnp.float32)
        taps_now = [jnp.broadcast_to(coef_ref[t : t + 1, lanes], (ROWS, LANES)) for t in range(taps)]
        first = frames - taps + 1
        totals = [None] * frames
        for row in range(first, 2 * frames):
            value = frames_ref[pl.ds(row, inputs, stride=2 * frames), :]
            for f in range(max(0, row - first - taps + 1), min(frames, row - first + 1)):
                term = taps_now[row - first - f] * value
                totals[f] = term if totals[f] is None else totals[f] + term
        for f in range(frames):
            kept_ref[block, pl.ds(f, inputs, stride=frames), :] = totals[f]
        return carry

    lax.fori_loop(0, length // LANES, one_block, 0, unroll=2)
    if following:

        @pl.when(step == 0)
        def _():
            fetch.wait()
            store.start()


    def one_rows(index, carry):
        part = index % parts
        first = pl.multiple_of(index // parts * 16, 16)
        values = [kept_ref[parts * j + part, pl.ds(first, 16), :] for j in range(RADIX)]
        bins = real_fourier(values)
        rows = pl.ds(pl.multiple_of(base + first, 16), 16)
        for group in range(GROUPS):
            pair = (bins[0][0], bins[GROUPS][0]) if group == 0 else bins[group]
            for half in range(2):
                lanes = pl.ds(pl.multiple_of(half * span + part * LANES, LANES), LANES)
                top = pair[half].astype(jnp.bfloat16)
                high_ref[group, rows, lanes] = top
                low_ref[group, rows, lanes] = (pair[half] - top.astype(jnp.float32)).astype(jnp.bfloat16)
        return carry

    lax.fori_loop(0, parts * inputs * frames // 16, one_rows, 0, unroll=4)

    @pl.when(step == steps - 1)
    def _():
        copy.wait()

        def one_group(group, carry):
            top, rest = high_ref[group], low_ref[group]
            total = jnp.dot(top, table_ref[group, 0], preferred_element_type=jnp.float32)
            total = total + jnp.dot(rest, table_ref[group, 0], preferred_element_type=jnp.float32)
            total = total + jnp.dot(top, table_ref[group, 1], preferred_element_type=jnp.float32)
            spec_ref[group] = total
            return carry

        lax.fori_loop(0, GROUPS, one_group, 0, unroll=GROUPS)
        owners = out_ref.shape[0]
        slots = GROUPS
        run = LANES // slots

        def one_part(index, carry):
            first = pl.multiple_of(index * 16, 16)
            slot = lax.broadcasted_iota(jnp.int32, (16, LANES), 1) // run
            picks = [(slot // (1 << bit)) % 2 == 1 for bit in range(3)]
            for kind in range(2):
                for block in range(owners // slots):
                    lanes = pl.ds((kind * (owners // slots) + block) * LANES, LANES)
                    now = [spec_ref[group, pl.ds(first, 16), lanes] for group in range(GROUPS)]
                    for bit in range(3):
                        now = [jnp.where(picks[bit], now[(e - (1 << bit)) % slots], now[e]) for e in range(slots)]
                    for inside in range(slots):
                        out_ref[block * slots + inside, pl.ds(first, 16), pl.ds(kind * LANES, LANES)] = now[inside].astype(jnp.bfloat16)
            return carry

        lax.fori_loop(0, out_ref.shape[1] // 16, one_part, 0, unroll=4)
        if following:
            store.wait()


def filter_bank(samples, history, coefficients, table, first, count, owners, following):
    _, frames, length = samples.shape
    steps = count // ROWS
    rows = count * frames
    offset = first // ROWS
    in_specs = [
        pl.BlockSpec((ROWS, frames, length), lambda i: (i + offset, 0, 0)),
        pl.BlockSpec(coefficients.shape, lambda i: (0, 0), pipeline_mode=pl.Buffered(1)),
        pl.BlockSpec(memory_space=pl.ANY),
        pl.BlockSpec(memory_space=pl.ANY),
    ]
    out_specs = [pl.BlockSpec((owners, rows, 2 * LANES), lambda i: (0, 0, 0), pipeline_mode=pl.Buffered(1))]
    out_shape = [jax.ShapeDtypeStruct((owners, rows, 2 * LANES), jnp.bfloat16)]
    operands = [samples, coefficients, table, history]
    if following:
        in_specs.append(pl.BlockSpec(memory_space=pl.ANY))
        out_specs.append(pl.BlockSpec(memory_space=pl.ANY))
        out_shape.append(jax.ShapeDtypeStruct((following[1], frames, length), samples.dtype))
        operands.append(samples)
    return pl.pallas_call(
        functools.partial(filter_bank_kernel, steps, following),
        out_shape=out_shape,
        grid=(steps,),
        in_specs=in_specs,
        out_specs=out_specs,
        scratch_shapes=[
            pltpu.VMEM((steps, ROWS, frames, length), jnp.bfloat16),
            pltpu.VMEM((2 * ROWS * frames, LANES), jnp.float32),
            pltpu.VMEM((length // LANES, ROWS * frames, LANES), jnp.float32),
            pltpu.VMEM((GROUPS, rows, 2 * length // RADIX), jnp.bfloat16),
            pltpu.VMEM((GROUPS, rows, 2 * length // RADIX), jnp.bfloat16),
            pltpu.VMEM((GROUPS, rows, 2 * owners * LANES // GROUPS), jnp.float32),
            pltpu.VMEM(table.shape, jnp.bfloat16),
            pltpu.SemaphoreType.DMA((steps + 3,)),
        ]
        + ([pltpu.VMEM((following[1], frames, length), samples.dtype)] if following else []),
        compiler_params=pltpu.CompilerParams(vmem_limit_bytes=62 * MIB),
        cost_estimate=pl.CostEstimate(flops=10**11, bytes_accessed=16 * MIB, transcendentals=0),
        name="filter_bank",
    )(*operands)


def cut_kernel(in_ref, out_ref):
    out_ref[...] = in_ref[...]


def cut(samples, first, count):
    block = (ROWS, *samples.shape[1:])
    return pl.pallas_call(
        cut_kernel,
        out_shape=jax.ShapeDtypeStruct((count, *samples.shape[1:]), samples.dtype),
        grid=(count // ROWS,),
        in_specs=[pl.BlockSpec(block, lambda i: (i + first // ROWS, 0, 0))],
        out_specs=pl.BlockSpec(block, lambda i: (i, 0, 0)),
        cost_estimate=pl.CostEstimate(flops=0, bytes_accessed=4 * MIB, transcendentals=0),
        name="cut",
    )(samples)


def turn_kernel(frames, in_ref, out_ref, work_ref):
    blocks, rows, _ = in_ref.shape
    count = rows // frames

    def one_input(i, carry):
        first = pl.multiple_of(i * frames, frames)
        pieces = [
            in_ref[t, pl.ds(first, frames), pl.ds(kind * LANES, LANES)]
            for kind in range(2)
            for t in range(blocks)
        ]
        square = jnp.concatenate(pieces, axis=0).astype(jnp.float32)
        work_ref[pl.ds(i, LANES, stride=count), :] = square.T
        return carry

    lax.fori_loop(0, count, one_input, 0, unroll=count)
    out_ref[...] = work_ref[...].reshape(LANES, count, LANES).astype(jnp.bfloat16)


def turn(arrived, sets, frames):
    sources, rows, _ = arrived.shape
    blocks = sources // sets
    count = rows // frames
    return pl.pallas_call(
        functools.partial(turn_kernel, frames),
        out_shape=jax.ShapeDtypeStruct((LANES, sets * count, LANES), jnp.bfloat16),
        grid=(sets,),
        in_specs=[pl.BlockSpec((blocks, rows, 2 * LANES), lambda z: (z, 0, 0))],
        out_specs=pl.BlockSpec((LANES, count, LANES), lambda z: (0, z, 0)),
        scratch_shapes=[pltpu.VMEM((LANES * count, LANES), jnp.float32)],
        compiler_params=pltpu.CompilerParams(vmem_limit_bytes=20 * MIB),
        cost_estimate=pl.CostEstimate(flops=4 * arrived.size, bytes_accessed=4 * arrived.size, transcendentals=0),
        name="turn",
    )(arrived)


def correlate_kernel(counts, sets, scale, order_ref, *refs):
    *in_refs, out_hbm, kept_ref, sems = refs
    _, many, held, width, _ = kept_ref.shape
    step = pl.program_id(0)
    slot = step % 2

    def copies(of_step, of_slot):
        return [
            pltpu.make_async_copy(
                kept_ref.at[of_slot, k], out_hbm.at[:, order_ref[many * of_step + k]], sems.at[of_slot, k]
            )
            for k in range(many)
        ]

    @pl.when(step >= 2)
    def _():
        for copy in copies(step - 2, slot):
            copy.wait()

    row = lax.broadcasted_iota(jnp.int32, (width, width), 0)
    col = lax.broadcasted_iota(jnp.int32, (width, width), 1)
    for k in range(many):
        for u in range(held):
            joined = jnp.concatenate(
                [
                    in_ref[held * k + u, pl.ds(z * count, count), :]
                    for z in range(sets)
                    for in_ref, count in zip(in_refs, counts)
                ],
                axis=0,
            )
            turned = jnp.concatenate([joined[:, LANES // 2 :], -joined[:, : LANES // 2]], axis=1)
            both = lax.dot_general(
                jnp.concatenate([joined, turned], axis=0),
                joined,
                (((1,), (1,)), ((), ())),
                preferred_element_type=jnp.float32,
            )
            kept_ref[slot, k, u] = jnp.where(row <= col, both[:width], both[width:]) * scale
    for copy in copies(step, slot):
        copy.start()

    @pl.when(step == pl.num_programs(0) - 1)
    def _():
        for copy in copies(step - 1, 1 - slot) + copies(step, slot):
            copy.wait()


def correlate_all(turned, counts, sets, order, scale):
    channels = turned[0].shape[0]
    held = channels // RADIX
    width = sets * sum(counts)
    many = 2
    out = pl.pallas_call(
        functools.partial(correlate_kernel, counts, sets, scale),
        out_shape=jax.ShapeDtypeStruct((held, RADIX, width, width), jnp.float32),
        grid_spec=pltpu.PrefetchScalarGridSpec(
            num_scalar_prefetch=1,
            grid=(RADIX // many,),
            in_specs=[
                pl.BlockSpec((many * held, sets * count, LANES), lambda s, order: (s, 0, 0)) for count in counts
            ],
            out_specs=pl.BlockSpec(memory_space=pl.ANY),
            scratch_shapes=[
                pltpu.VMEM((2, many, held, width, width), jnp.float32),
                pltpu.SemaphoreType.DMA((2, many)),
            ],
        ),
        compiler_params=pltpu.CompilerParams(vmem_limit_bytes=36 * MIB),
        cost_estimate=pl.CostEstimate(
            flops=4 * channels * width * width * LANES, bytes_accessed=40 * MIB, transcendentals=0
        ),
        name="correlate",
    )(order, *turned)
    return out.reshape(channels, width, width)


def plan(in_dev):
    units = in_dev // ROWS
    return [ROWS * size for size in (1, 2, 2, units - 5)]


def fast(samples, coefficients):
    in_dev, frames, length = samples.shape
    everyone = ("inp", "tm", "pol")
    owners = lax.axis_size(everyone)
    sets = lax.axis_size("inp")
    total_frames = frames * owners // sets
    table = jnp.asarray(fourier_tables(length, owners))
    counts = plan(in_dev)
    starts = [sum(counts[:k]) for k in range(len(counts))]
    slot = lax.axis_index(everyone) % GROUPS
    steps = jnp.arange(RADIX, dtype=jnp.int32)
    group, side = (slot - steps // 2) % GROUPS, steps % 2
    order = jnp.where(group == 0, side * GROUPS, jnp.where(side == 0, group, RADIX - group)).astype(jnp.int32)
    last = len(counts) - 1
    parts = list(zip(starts, counts))
    histories = [from_behind(samples[: counts[0]], ("tm", "pol"), 1)]
    piece, histories[0] = lax.optimization_barrier((cut(samples, *parts[1]), histories[0]))
    histories.append(from_behind(piece, ("tm", "pol"), 1))
    turned = []
    for k in range(last + 1):
        following = parts[k + 2] if k + 2 <= last else None
        spectra, *pieces = filter_bank(
            samples, histories[k], coefficients, table, starts[k], counts[k], owners, following
        )
        if following:
            piece = pieces[0]
            if k > 0:
                piece, arrived = lax.optimization_barrier((piece, arrived))
            piece, histories[k + 1] = lax.optimization_barrier((piece, histories[k + 1]))
            histories.append(from_behind(piece, ("tm", "pol"), 1))
        if k > 0:
            turned.append(turn(arrived, sets, frames))
        arrived = lax.all_to_all(spectra, everyone, 0, 0, tiled=True)
    turned.append(turn(arrived, sets, frames))
    return correlate_all(turned, counts, sets, order, 1.0 / total_frames)


def per_device(samples, coefficients):
    in_dev, frames, length = samples.shape
    taps = coefficients.shape[0]
    owners = lax.axis_size(("inp", "tm", "pol"))
    blocks = lax.axis_size(("tm", "pol"))
    fits = (
        frames == 16
        and taps <= frames + 1
        and in_dev % (4 * ROWS) == 0
        and length == 2 * LANES * owners
        and length % (RADIX * LANES) == 0
        and owners % GROUPS == 0
        and 2 * blocks * frames == LANES
    )
    return fast(samples, coefficients) if fits else general(samples, coefficients)


def solution(mesh):
    placed = (P(("grp", "inp"), ("tm", "pol"), None), P())
    return jax.shard_map(
        per_device,
        mesh=mesh,
        in_specs=placed,
        out_specs=P(("grp", "inp", "tm", "pol"), None, None),
        check_vma=False,
    )
```

```python
import functools
import math

import jax
import jax.numpy as jnp
import ml_dtypes
import numpy as np
from jax import lax
from jax.experimental import pallas as pl
from jax.experimental.pallas import tpu as pltpu
from jax.sharding import PartitionSpec as P

RADIX = 16
GROUPS = RADIX // 2
LANES = 128
ROWS = 8
MIB = 1 << 20


def from_behind(block, axis, distance):
    devices = range(lax.axis_size(axis))
    route = [(i - distance, i) for i in devices if i - distance in devices]
    return lax.ppermute(block, axis, route)


def correlate(real_part, imag_part, total_frames):
    joined = jnp.concatenate([real_part, imag_part], axis=2)
    turned = jnp.concatenate([imag_part, -real_part], axis=2)
    stacked = jnp.concatenate([joined, turned], axis=1)
    product = jnp.einsum("cif,cjf->cij", stacked, joined, preferred_element_type=jnp.float32)
    width = real_part.shape[1]
    row_index = lax.broadcasted_iota(jnp.int32, (width, width), 0)
    col_index = lax.broadcasted_iota(jnp.int32, (width, width), 1)
    packed = jnp.where(row_index <= col_index, product[:, :width], product[:, width:])
    return packed * (1.0 / total_frames)


def filter_frames(block, coefficients, taps):
    frame_count = block.shape[1] - taps + 1
    total = jnp.zeros((block.shape[0], frame_count, block.shape[2]), jnp.float32)
    for tap_index in range(taps):
        total = total + coefficients[tap_index] * block[
            :, tap_index : tap_index + frame_count
        ].astype(jnp.float32)
    return total


def angles(first_idx, second_idx, period):
    product = first_idx[:, None] * second_idx[None, :] % period
    return product.astype(jnp.float32) * (2.0 * math.pi / period)


def transform(filtered):
    row_total, length = filtered.shape
    inner_len = 2 ** ((length.bit_length() - 1) // 2)
    outer_len = length // inner_len
    blocks = filtered.reshape(row_total, inner_len, outer_len)
    inner_idx = jnp.arange(inner_len, dtype=jnp.int32)
    outer_idx = jnp.arange(outer_len, dtype=jnp.int32)
    half_idx = jnp.arange(outer_len // 2, dtype=jnp.int32)
    angle_one = angles(inner_idx, inner_idx, inner_len)
    table_one = jnp.concatenate([jnp.cos(angle_one), -jnp.sin(angle_one)], axis=1)
    section_one = jnp.einsum("rab,ak->rbk", blocks, table_one, precision=lax.Precision.HIGHEST)
    first_re = section_one[..., :inner_len]
    first_im = section_one[..., inner_len:]
    angle_twist = angles(outer_idx, inner_idx, length)
    twist_cos = jnp.cos(angle_twist)
    twist_sin = jnp.sin(angle_twist)
    turned_re = first_re * twist_cos + first_im * twist_sin
    turned_im = first_im * twist_cos - first_re * twist_sin
    angle_two = angles(outer_idx, half_idx, outer_len)
    table_cos = jnp.cos(angle_two)
    table_sin = jnp.sin(angle_two)
    highest = lax.Precision.HIGHEST
    out_re = jnp.einsum("rbk,bq->qkr", turned_re, table_cos, precision=highest) + jnp.einsum(
        "rbk,bq->qkr", turned_im, table_sin, precision=highest
    )
    out_im = jnp.einsum("rbk,bq->qkr", turned_im, table_cos, precision=highest) - jnp.einsum(
        "rbk,bq->qkr", turned_re, table_sin, precision=highest
    )
    scale_factor = 1.0 / math.sqrt(length)
    return jnp.stack([out_re, out_im]).reshape(2, length // 2, row_total) * scale_factor


def general(samples, coefficients):
    in_dev, frame_count, length = samples.shape
    taps = coefficients.shape[0]
    channels = length // 2
    history = from_behind(samples[:, frame_count - taps + 1 :, :], ("tm", "pol"), 1)
    extended = jnp.concatenate([history, samples], axis=1)
    group_size = math.gcd(in_dev, 4)
    spectra_buf = jnp.zeros((2, channels, in_dev, frame_count), jnp.bfloat16)

    def one_group(group_index, buffer_now):
        block = lax.dynamic_slice_in_dim(extended, group_index * group_size, group_size, 0)
        filtered = filter_frames(block, coefficients, taps).reshape(
            group_size * frame_count, length
        )
        spectra_grp = (
            transform(filtered).reshape(2, channels, group_size, frame_count).astype(jnp.bfloat16)
        )
        return lax.dynamic_update_slice_in_dim(buffer_now, spectra_grp, group_index * group_size, 2)

    local_spec = lax.fori_loop(0, in_dev // group_size, one_group, spectra_buf)
    n_inputs = lax.axis_size("inp")
    n_blocks = lax.axis_size("tm")
    n_halves = lax.axis_size("pol")
    total_frames = frame_count * n_blocks * n_halves
    arrived = lax.all_to_all(
        local_spec[None], ("inp", "tm", "pol"), split_axis=2, concat_axis=0, tiled=True
    )
    width = arrived.shape[2]
    arrived = arrived.reshape(n_inputs, n_blocks * n_halves, 2, width, in_dev, frame_count)
    arrived = jnp.transpose(arrived, (2, 3, 0, 4, 1, 5)).reshape(
        2, width, n_inputs * in_dev, n_blocks * n_halves * frame_count
    )
    return correlate(arrived[0], arrived[1], total_frames)


@functools.lru_cache(maxsize=None)
def fourier_tables(length, owners):
    span = length // RADIX
    per_owner = length // 2 // owners // RADIX
    run = 2 * per_owner
    slots = LANES // run
    place = np.arange(span, dtype=np.int64)
    tables = np.zeros((GROUPS, 2 * span, 2 * owners * run))
    for group in range(GROUPS):
        for owner in range(owners):
            block, inside = divmod(owner, slots)
            column = block * LANES + ((inside - group) % slots) * run
            for side in range(2):
                residue = side * GROUPS if group == 0 else (group, RADIX - group)[side]
                channel = RADIX * (owner * per_owner + np.arange(per_owner)) + residue
                angle = 2.0 * np.pi * (place[:, None] * channel[None, :] % length) / length
                cos, sin = np.cos(angle) / math.sqrt(length), np.sin(angle) / math.sqrt(length)
                re = slice(column + side * per_owner, column + (side + 1) * per_owner)
                im = slice(re.start + owners * run, re.stop + owners * run)
                if group == 0:
                    rows = slice(side * span, (side + 1) * span)
                    tables[group, rows, re] = cos
                    tables[group, rows, im] = -sin
                else:
                    sign = 1.0 - 2.0 * side
                    tables[group, :span, re] = cos
                    tables[group, span:, re] = sign * sin
                    tables[group, :span, im] = -sin
                    tables[group, span:, im] = sign * cos
    exact = tables.astype(np.float32)
    high = exact.astype(ml_dtypes.bfloat16)
    low = (exact - high.astype(np.float32)).astype(ml_dtypes.bfloat16)
    return np.stack([high, low], axis=1)


def real_fourier(values):
    count = len(values)
    if count == 1:
        return [(values[0], None)]
    if count == 2:
        return [(values[0] + values[1], None), (values[0] - values[1], None)]
    even, odd = real_fourier(values[0::2]), real_fourier(values[1::2])
    bins = [None] * (count // 2 + 1)
    bins[0] = (even[0][0] + odd[0][0], None)
    bins[count // 2] = (even[0][0] - odd[0][0], None)
    bins[count // 4] = (even[count // 4][0], -odd[count // 4][0])
    for k in range(1, count // 4):
        (er, ei), (pr, pi) = even[k], odd[k]
        if 8 * k == count:
            half = math.sqrt(0.5)
            tr, ti = (pr + pi) * half, (pi - pr) * half
        else:
            c, s = math.cos(2 * math.pi * k / count), math.sin(2 * math.pi * k / count)
            tr, ti = pr * c + pi * s, pi * c - pr * s
        bins[k] = (er + tr, ei + ti)
        bins[count // 2 - k] = (er - tr, ti - ei)
    return bins


def filter_bank_kernel(steps, following, own_ref, coef_ref, table_hbm, history_hbm, *refs):
    if following:
        samples_hbm, out_ref, piece_hbm, *refs, piece_ref = refs
        fetch = pltpu.make_async_copy(samples_hbm.at[pl.ds(*following)], piece_ref, refs[-1].at[steps + 1])
        store = pltpu.make_async_copy(piece_ref, piece_hbm, refs[-1].at[steps + 2])
    else:
        out_ref, *refs = refs
    past_ref, frames_ref, kept_ref, high_ref, low_ref, spec_ref, table_ref, sems = refs
    inputs, frames, length = own_ref.shape
    taps = coef_ref.shape[0]
    span = length // RADIX
    parts = span // LANES
    step = pl.program_id(0)
    copy = pltpu.make_async_copy(table_hbm, table_ref, sems.at[steps])

    @pl.when(step == 0)
    def _():
        for k in range(steps):
            pltpu.make_async_copy(history_hbm.at[pl.ds(k * inputs, inputs)], past_ref.at[k], sems.at[k]).start()
        copy.start()
        if following:
            fetch.start()

    for k in range(steps):

        @pl.when(step == k)
        def _():
            pltpu.make_async_copy(history_hbm.at[pl.ds(k * inputs, inputs)], past_ref.at[k], sems.at[k]).wait()

    base = step * inputs * frames

    def one_block(block, carry):
        lanes = pl.ds(pl.multiple_of(block * LANES, LANES), LANES)
        for i in range(inputs):
            frames_ref[pl.ds(2 * frames * i, frames), :] = past_ref[step, i, :, lanes].astype(jnp.float32)
            frames_ref[pl.ds(2 * frames * i + frames, frames), :] = own_ref[i, :, lanes].astype(jnp.float32)
        taps_now = [jnp.broadcast_to(coef_ref[t : t + 1, lanes], (ROWS, LANES)) for t in range(taps)]
        first = frames - taps + 1
        totals = [None] * frames
        for row in range(first, 2 * frames):
            value = frames_ref[pl.ds(row, inputs, stride=2 * frames), :]
            for f in range(max(0, row - first - taps + 1), min(frames, row - first + 1)):
                term = taps_now[row - first - f] * value
                totals[f] = term if totals[f] is None else totals[f] + term
        for f in range(frames):
            kept_ref[block, pl.ds(f, inputs, stride=frames), :] = totals[f]
        return carry

    lax.fori_loop(0, length // LANES, one_block, 0, unroll=2)
    if following:

        @pl.when(step == 0)
        def _():
            fetch.wait()
            store.start()


    def one_rows(index, carry):
        part = index % parts
        first = pl.multiple_of(index // parts * 16, 16)
        values = [kept_ref[parts * j + part, pl.ds(first, 16), :] for j in range(RADIX)]
        bins = real_fourier(values)
        rows = pl.ds(pl.multiple_of(base + first, 16), 16)
        for group in range(GROUPS):
            pair = (bins[0][0], bins[GROUPS][0]) if group == 0 else bins[group]
            for half in range(2):
                lanes = pl.ds(pl.multiple_of(half * span + part * LANES, LANES), LANES)
                top = pair[half].astype(jnp.bfloat16)
                high_ref[group, rows, lanes] = top
                low_ref[group, rows, lanes] = (pair[half] - top.astype(jnp.float32)).astype(jnp.bfloat16)
        return carry

    lax.fori_loop(0, parts * inputs * frames // 16, one_rows, 0, unroll=4)

    @pl.when(step == steps - 1)
    def _():
        copy.wait()

        def one_group(group, carry):
            top, rest = high_ref[group], low_ref[group]
            total = jnp.dot(top, table_ref[group, 0], preferred_element_type=jnp.float32)
            total = total + jnp.dot(rest, table_ref[group, 0], preferred_element_type=jnp.float32)
            total = total + jnp.dot(top, table_ref[group, 1], preferred_element_type=jnp.float32)
            spec_ref[group] = total
            return carry

        lax.fori_loop(0, GROUPS, one_group, 0, unroll=GROUPS)
        owners = out_ref.shape[0]
        slots = GROUPS
        run = LANES // slots

        def one_part(index, carry):
            first = pl.multiple_of(index * 16, 16)
            slot = lax.broadcasted_iota(jnp.int32, (16, LANES), 1) // run
            picks = [(slot // (1 << bit)) % 2 == 1 for bit in range(3)]
            for kind in range(2):
                for block in range(owners // slots):
                    lanes = pl.ds((kind * (owners // slots) + block) * LANES, LANES)
                    now = [spec_ref[group, pl.ds(first, 16), lanes] for group in range(GROUPS)]
                    for bit in range(3):
                        now = [jnp.where(picks[bit], now[(e - (1 << bit)) % slots], now[e]) for e in range(slots)]
                    for inside in range(slots):
                        out_ref[block * slots + inside, pl.ds(first, 16), pl.ds(kind * LANES, LANES)] = now[inside].astype(jnp.bfloat16)
            return carry

        lax.fori_loop(0, out_ref.shape[1] // 16, one_part, 0, unroll=4)
        if following:
            store.wait()


def filter_bank(samples, history, coefficients, table, first, count, owners, following):
    _, frames, length = samples.shape
    steps = count // ROWS
    rows = count * frames
    offset = first // ROWS
    in_specs = [
        pl.BlockSpec((ROWS, frames, length), lambda i: (i + offset, 0, 0)),
        pl.BlockSpec(coefficients.shape, lambda i: (0, 0), pipeline_mode=pl.Buffered(1)),
        pl.BlockSpec(memory_space=pl.ANY),
        pl.BlockSpec(memory_space=pl.ANY),
    ]
    out_specs = [pl.BlockSpec((owners, rows, 2 * LANES), lambda i: (0, 0, 0), pipeline_mode=pl.Buffered(1))]
    out_shape = [jax.ShapeDtypeStruct((owners, rows, 2 * LANES), jnp.bfloat16)]
    operands = [samples, coefficients, table, history]
    if following:
        in_specs.append(pl.BlockSpec(memory_space=pl.ANY))
        out_specs.append(pl.BlockSpec(memory_space=pl.ANY))
        out_shape.append(jax.ShapeDtypeStruct((following[1], frames, length), samples.dtype))
        operands.append(samples)
    return pl.pallas_call(
        functools.partial(filter_bank_kernel, steps, following),
        out_shape=out_shape,
        grid=(steps,),
        in_specs=in_specs,
        out_specs=out_specs,
        scratch_shapes=[
            pltpu.VMEM((steps, ROWS, frames, length), jnp.bfloat16),
            pltpu.VMEM((2 * ROWS * frames, LANES), jnp.float32),
            pltpu.VMEM((length // LANES, ROWS * frames, LANES), jnp.float32),
            pltpu.VMEM((GROUPS, rows, 2 * length // RADIX), jnp.bfloat16),
            pltpu.VMEM((GROUPS, rows, 2 * length // RADIX), jnp.bfloat16),
            pltpu.VMEM((GROUPS, rows, 2 * owners * LANES // GROUPS), jnp.float32),
            pltpu.VMEM(table.shape, jnp.bfloat16),
            pltpu.SemaphoreType.DMA((steps + 3,)),
        ]
        + ([pltpu.VMEM((following[1], frames, length), samples.dtype)] if following else []),
        compiler_params=pltpu.CompilerParams(vmem_limit_bytes=63 * MIB),
        cost_estimate=pl.CostEstimate(flops=10**11, bytes_accessed=16 * MIB, transcendentals=0),
        name="filter_bank",
    )(*operands)


def cut_kernel(in_ref, out_ref):
    out_ref[...] = in_ref[...]


def cut(samples, first, count):
    block = (ROWS, *samples.shape[1:])
    return pl.pallas_call(
        cut_kernel,
        out_shape=jax.ShapeDtypeStruct((count, *samples.shape[1:]), samples.dtype),
        grid=(count // ROWS,),
        in_specs=[pl.BlockSpec(block, lambda i: (i + first // ROWS, 0, 0))],
        out_specs=pl.BlockSpec(block, lambda i: (i, 0, 0)),
        cost_estimate=pl.CostEstimate(flops=0, bytes_accessed=4 * MIB, transcendentals=0),
        name="cut",
    )(samples)


def turn_kernel(frames, in_ref, out_ref, work_ref):
    blocks, rows, _ = in_ref.shape
    count = rows // frames

    def one_input(i, carry):
        first = pl.multiple_of(i * frames, frames)
        pieces = [
            in_ref[t, pl.ds(first, frames), pl.ds(kind * LANES, LANES)]
            for kind in range(2)
            for t in range(blocks)
        ]
        square = jnp.concatenate(pieces, axis=0).astype(jnp.float32)
        work_ref[pl.ds(i, LANES, stride=count), :] = square.T
        return carry

    lax.fori_loop(0, count, one_input, 0, unroll=count)
    out_ref[...] = work_ref[...].reshape(LANES, count, LANES).astype(jnp.bfloat16)


def turn(arrived, sets, frames):
    sources, rows, _ = arrived.shape
    blocks = sources // sets
    count = rows // frames
    return pl.pallas_call(
        functools.partial(turn_kernel, frames),
        out_shape=jax.ShapeDtypeStruct((LANES, sets * count, LANES), jnp.bfloat16),
        grid=(sets,),
        in_specs=[pl.BlockSpec((blocks, rows, 2 * LANES), lambda z: (z, 0, 0))],
        out_specs=pl.BlockSpec((LANES, count, LANES), lambda z: (0, z, 0)),
        scratch_shapes=[pltpu.VMEM((LANES * count, LANES), jnp.float32)],
        compiler_params=pltpu.CompilerParams(vmem_limit_bytes=20 * MIB),
        cost_estimate=pl.CostEstimate(flops=4 * arrived.size, bytes_accessed=4 * arrived.size, transcendentals=0),
        name="turn",
    )(arrived)


def correlate_kernel(counts, sets, scale, order_ref, *refs):
    *in_refs, out_hbm, kept_ref, sems = refs
    _, many, held, width, _ = kept_ref.shape
    step = pl.program_id(0)
    slot = step % 2

    def copies(of_step, of_slot):
        return [
            pltpu.make_async_copy(
                kept_ref.at[of_slot, k], out_hbm.at[:, order_ref[many * of_step + k]], sems.at[of_slot, k]
            )
            for k in range(many)
        ]

    @pl.when(step >= 2)
    def _():
        for copy in copies(step - 2, slot):
            copy.wait()

    row = lax.broadcasted_iota(jnp.int32, (width, width), 0)
    col = lax.broadcasted_iota(jnp.int32, (width, width), 1)
    for k in range(many):
        for u in range(held):
            joined = jnp.concatenate(
                [
                    in_ref[held * k + u, pl.ds(z * count, count), :]
                    for z in range(sets)
                    for in_ref, count in zip(in_refs, counts)
                ],
                axis=0,
            )
            turned = jnp.concatenate([joined[:, LANES // 2 :], -joined[:, : LANES // 2]], axis=1)
            both = lax.dot_general(
                jnp.concatenate([joined, turned], axis=0),
                joined,
                (((1,), (1,)), ((), ())),
                preferred_element_type=jnp.float32,
            )
            kept_ref[slot, k, u] = jnp.where(row <= col, both[:width], both[width:]) * scale
    for copy in copies(step, slot):
        copy.start()

    @pl.when(step == pl.num_programs(0) - 1)
    def _():
        for copy in copies(step - 1, 1 - slot) + copies(step, slot):
            copy.wait()


def correlate_all(turned, counts, sets, order, scale):
    channels = turned[0].shape[0]
    held = channels // RADIX
    width = sets * sum(counts)
    many = 4
    out = pl.pallas_call(
        functools.partial(correlate_kernel, counts, sets, scale),
        out_shape=jax.ShapeDtypeStruct((held, RADIX, width, width), jnp.float32),
        grid_spec=pltpu.PrefetchScalarGridSpec(
            num_scalar_prefetch=1,
            grid=(RADIX // many,),
            in_specs=[
                pl.BlockSpec((many * held, sets * count, LANES), lambda s, order: (s, 0, 0)) for count in counts
            ],
            out_specs=pl.BlockSpec(memory_space=pl.ANY),
            scratch_shapes=[
                pltpu.VMEM((2, many, held, width, width), jnp.float32),
                pltpu.SemaphoreType.DMA((2, many)),
            ],
        ),
        compiler_params=pltpu.CompilerParams(vmem_limit_bytes=36 * MIB),
        cost_estimate=pl.CostEstimate(
            flops=4 * channels * width * width * LANES, bytes_accessed=40 * MIB, transcendentals=0
        ),
        name="correlate",
    )(order, *turned)
    return out.reshape(channels, width, width)


def plan(in_dev):
    units = in_dev // ROWS
    return [ROWS * size for size in (1, 2, 2, units - 5)]


def fast(samples, coefficients):
    in_dev, frames, length = samples.shape
    everyone = ("inp", "tm", "pol")
    owners = lax.axis_size(everyone)
    sets = lax.axis_size("inp")
    total_frames = frames * owners // sets
    table = jnp.asarray(fourier_tables(length, owners))
    counts = plan(in_dev)
    starts = [sum(counts[:k]) for k in range(len(counts))]
    slot = lax.axis_index(everyone) % GROUPS
    steps = jnp.arange(RADIX, dtype=jnp.int32)
    group, side = (slot - steps // 2) % GROUPS, steps % 2
    order = jnp.where(group == 0, side * GROUPS, jnp.where(side == 0, group, RADIX - group)).astype(jnp.int32)
    last = len(counts) - 1
    parts = list(zip(starts, counts))
    histories = [from_behind(samples[: counts[0]], ("tm", "pol"), 1)]
    piece, histories[0] = lax.optimization_barrier((cut(samples, *parts[1]), histories[0]))
    histories.append(from_behind(piece, ("tm", "pol"), 1))
    turned = []
    for k in range(last + 1):
        following = parts[k + 2] if k + 2 <= last else None
        spectra, *pieces = filter_bank(
            samples, histories[k], coefficients, table, starts[k], counts[k], owners, following
        )
        if following:
            piece = pieces[0]
            if k > 0:
                piece, arrived = lax.optimization_barrier((piece, arrived))
            piece, histories[k + 1] = lax.optimization_barrier((piece, histories[k + 1]))
            histories.append(from_behind(piece, ("tm", "pol"), 1))
        if k > 0:
            turned.append(turn(arrived, sets, frames))
        arrived = lax.all_to_all(spectra, everyone, 0, 0, tiled=True)
    turned.append(turn(arrived, sets, frames))
    return correlate_all(turned, counts, sets, order, 1.0 / total_frames)


def per_device(samples, coefficients):
    in_dev, frames, length = samples.shape
    taps = coefficients.shape[0]
    owners = lax.axis_size(("inp", "tm", "pol"))
    blocks = lax.axis_size(("tm", "pol"))
    fits = (
        frames == 16
        and taps <= frames + 1
        and in_dev % (4 * ROWS) == 0
        and length == 2 * LANES * owners
        and length % (RADIX * LANES) == 0
        and owners % GROUPS == 0
        and 2 * blocks * frames == LANES
    )
    return fast(samples, coefficients) if fits else general(samples, coefficients)


def solution(mesh):
    placed = (P(("grp", "inp"), ("tm", "pol"), None), P())
    return jax.shard_map(
        per_device,
        mesh=mesh,
        in_specs=placed,
        out_specs=P(("grp", "inp", "tm", "pol"), None, None),
        check_vma=False,
    )
```

```python
import functools
import math

import jax
import jax.numpy as jnp
import ml_dtypes
import numpy as np
from jax import lax
from jax.experimental import pallas as pl
from jax.experimental.pallas import tpu as pltpu
from jax.sharding import PartitionSpec as P

RADIX = 16
GROUPS = RADIX // 2
LANES = 128
ROWS = 8
MIB = 1 << 20


def from_behind(block, axis, distance):
    devices = range(lax.axis_size(axis))
    route = [(i - distance, i) for i in devices if i - distance in devices]
    return lax.ppermute(block, axis, route)


def correlate(real_part, imag_part, total_frames):
    joined = jnp.concatenate([real_part, imag_part], axis=2)
    turned = jnp.concatenate([imag_part, -real_part], axis=2)
    stacked = jnp.concatenate([joined, turned], axis=1)
    product = jnp.einsum("cif,cjf->cij", stacked, joined, preferred_element_type=jnp.float32)
    width = real_part.shape[1]
    row_index = lax.broadcasted_iota(jnp.int32, (width, width), 0)
    col_index = lax.broadcasted_iota(jnp.int32, (width, width), 1)
    packed = jnp.where(row_index <= col_index, product[:, :width], product[:, width:])
    return packed * (1.0 / total_frames)


def filter_frames(block, coefficients, taps):
    frame_count = block.shape[1] - taps + 1
    total = jnp.zeros((block.shape[0], frame_count, block.shape[2]), jnp.float32)
    for tap_index in range(taps):
        total = total + coefficients[tap_index] * block[
            :, tap_index : tap_index + frame_count
        ].astype(jnp.float32)
    return total


def angles(first_idx, second_idx, period):
    product = first_idx[:, None] * second_idx[None, :] % period
    return product.astype(jnp.float32) * (2.0 * math.pi / period)


def transform(filtered):
    row_total, length = filtered.shape
    inner_len = 2 ** ((length.bit_length() - 1) // 2)
    outer_len = length // inner_len
    blocks = filtered.reshape(row_total, inner_len, outer_len)
    inner_idx = jnp.arange(inner_len, dtype=jnp.int32)
    outer_idx = jnp.arange(outer_len, dtype=jnp.int32)
    half_idx = jnp.arange(outer_len // 2, dtype=jnp.int32)
    angle_one = angles(inner_idx, inner_idx, inner_len)
    table_one = jnp.concatenate([jnp.cos(angle_one), -jnp.sin(angle_one)], axis=1)
    section_one = jnp.einsum("rab,ak->rbk", blocks, table_one, precision=lax.Precision.HIGHEST)
    first_re = section_one[..., :inner_len]
    first_im = section_one[..., inner_len:]
    angle_twist = angles(outer_idx, inner_idx, length)
    twist_cos = jnp.cos(angle_twist)
    twist_sin = jnp.sin(angle_twist)
    turned_re = first_re * twist_cos + first_im * twist_sin
    turned_im = first_im * twist_cos - first_re * twist_sin
    angle_two = angles(outer_idx, half_idx, outer_len)
    table_cos = jnp.cos(angle_two)
    table_sin = jnp.sin(angle_two)
    highest = lax.Precision.HIGHEST
    out_re = jnp.einsum("rbk,bq->qkr", turned_re, table_cos, precision=highest) + jnp.einsum(
        "rbk,bq->qkr", turned_im, table_sin, precision=highest
    )
    out_im = jnp.einsum("rbk,bq->qkr", turned_im, table_cos, precision=highest) - jnp.einsum(
        "rbk,bq->qkr", turned_re, table_sin, precision=highest
    )
    scale_factor = 1.0 / math.sqrt(length)
    return jnp.stack([out_re, out_im]).reshape(2, length // 2, row_total) * scale_factor


def general(samples, coefficients):
    in_dev, frame_count, length = samples.shape
    taps = coefficients.shape[0]
    channels = length // 2
    history = from_behind(samples[:, frame_count - taps + 1 :, :], ("tm", "pol"), 1)
    extended = jnp.concatenate([history, samples], axis=1)
    group_size = math.gcd(in_dev, 4)
    spectra_buf = jnp.zeros((2, channels, in_dev, frame_count), jnp.bfloat16)

    def one_group(group_index, buffer_now):
        block = lax.dynamic_slice_in_dim(extended, group_index * group_size, group_size, 0)
        filtered = filter_frames(block, coefficients, taps).reshape(
            group_size * frame_count, length
        )
        spectra_grp = (
            transform(filtered).reshape(2, channels, group_size, frame_count).astype(jnp.bfloat16)
        )
        return lax.dynamic_update_slice_in_dim(buffer_now, spectra_grp, group_index * group_size, 2)

    local_spec = lax.fori_loop(0, in_dev // group_size, one_group, spectra_buf)
    n_inputs = lax.axis_size("inp")
    n_blocks = lax.axis_size("tm")
    n_halves = lax.axis_size("pol")
    total_frames = frame_count * n_blocks * n_halves
    arrived = lax.all_to_all(
        local_spec[None], ("inp", "tm", "pol"), split_axis=2, concat_axis=0, tiled=True
    )
    width = arrived.shape[2]
    arrived = arrived.reshape(n_inputs, n_blocks * n_halves, 2, width, in_dev, frame_count)
    arrived = jnp.transpose(arrived, (2, 3, 0, 4, 1, 5)).reshape(
        2, width, n_inputs * in_dev, n_blocks * n_halves * frame_count
    )
    return correlate(arrived[0], arrived[1], total_frames)


@functools.lru_cache(maxsize=None)
def fourier_tables(length, owners):
    span = length // RADIX
    per_owner = length // 2 // owners // RADIX
    run = 2 * per_owner
    slots = LANES // run
    place = np.arange(span, dtype=np.int64)
    tables = np.zeros((GROUPS, 2 * span, 2 * owners * run))
    for group in range(GROUPS):
        for owner in range(owners):
            block, inside = divmod(owner, slots)
            column = block * LANES + ((inside - group) % slots) * run
            for side in range(2):
                residue = side * GROUPS if group == 0 else (group, RADIX - group)[side]
                channel = RADIX * (owner * per_owner + np.arange(per_owner)) + residue
                angle = 2.0 * np.pi * (place[:, None] * channel[None, :] % length) / length
                cos, sin = np.cos(angle) / math.sqrt(length), np.sin(angle) / math.sqrt(length)
                re = slice(column + side * per_owner, column + (side + 1) * per_owner)
                im = slice(re.start + owners * run, re.stop + owners * run)
                if group == 0:
                    rows = slice(side * span, (side + 1) * span)
                    tables[group, rows, re] = cos
                    tables[group, rows, im] = -sin
                else:
                    sign = 1.0 - 2.0 * side
                    tables[group, :span, re] = cos
                    tables[group, span:, re] = sign * sin
                    tables[group, :span, im] = -sin
                    tables[group, span:, im] = sign * cos
    exact = tables.astype(np.float32)
    high = exact.astype(ml_dtypes.bfloat16)
    low = (exact - high.astype(np.float32)).astype(ml_dtypes.bfloat16)
    return np.stack([high, low], axis=1)


def real_fourier(values):
    count = len(values)
    if count == 1:
        return [(values[0], None)]
    if count == 2:
        return [(values[0] + values[1], None), (values[0] - values[1], None)]
    even, odd = real_fourier(values[0::2]), real_fourier(values[1::2])
    bins = [None] * (count // 2 + 1)
    bins[0] = (even[0][0] + odd[0][0], None)
    bins[count // 2] = (even[0][0] - odd[0][0], None)
    bins[count // 4] = (even[count // 4][0], -odd[count // 4][0])
    for k in range(1, count // 4):
        (er, ei), (pr, pi) = even[k], odd[k]
        if 8 * k == count:
            half = math.sqrt(0.5)
            tr, ti = (pr + pi) * half, (pi - pr) * half
        else:
            c, s = math.cos(2 * math.pi * k / count), math.sin(2 * math.pi * k / count)
            tr, ti = pr * c + pi * s, pi * c - pr * s
        bins[k] = (er + tr, ei + ti)
        bins[count // 2 - k] = (er - tr, ti - ei)
    return bins


def filter_bank_kernel(steps, following, own_ref, coef_ref, table_hbm, history_hbm, *refs):
    if following:
        samples_hbm, out_ref, piece_hbm, *refs, piece_ref = refs
        fetch = pltpu.make_async_copy(samples_hbm.at[pl.ds(*following)], piece_ref, refs[-1].at[steps + 1])
        store = pltpu.make_async_copy(piece_ref, piece_hbm, refs[-1].at[steps + 2])
    else:
        out_ref, *refs = refs
    past_ref, frames_ref, kept_ref, high_ref, low_ref, spec_ref, table_ref, sems = refs
    inputs, frames, length = own_ref.shape
    taps = coef_ref.shape[0]
    span = length // RADIX
    parts = span // LANES
    step = pl.program_id(0)
    copy = pltpu.make_async_copy(table_hbm, table_ref, sems.at[steps])

    @pl.when(step == 0)
    def _():
        for k in range(steps):
            pltpu.make_async_copy(history_hbm.at[pl.ds(k * inputs, inputs)], past_ref.at[k], sems.at[k]).start()
        copy.start()
        if following:
            fetch.start()

    for k in range(steps):

        @pl.when(step == k)
        def _():
            pltpu.make_async_copy(history_hbm.at[pl.ds(k * inputs, inputs)], past_ref.at[k], sems.at[k]).wait()

    base = step * inputs * frames

    def one_block(block, carry):
        lanes = pl.ds(pl.multiple_of(block * LANES, LANES), LANES)
        for i in range(inputs):
            frames_ref[pl.ds(2 * frames * i, frames), :] = past_ref[step, i, :, lanes].astype(jnp.float32)
            frames_ref[pl.ds(2 * frames * i + frames, frames), :] = own_ref[i, :, lanes].astype(jnp.float32)
        taps_now = [jnp.broadcast_to(coef_ref[t : t + 1, lanes], (ROWS, LANES)) for t in range(taps)]
        first = frames - taps + 1
        totals = [None] * frames
        for row in range(first, 2 * frames):
            value = frames_ref[pl.ds(row, inputs, stride=2 * frames), :]
            for f in range(max(0, row - first - taps + 1), min(frames, row - first + 1)):
                term = taps_now[row - first - f] * value
                totals[f] = term if totals[f] is None else totals[f] + term
        for f in range(frames):
            kept_ref[block, pl.ds(f, inputs, stride=frames), :] = totals[f]
        return carry

    lax.fori_loop(0, length // LANES, one_block, 0, unroll=4)
    if following:

        @pl.when(step == 0)
        def _():
            fetch.wait()
            store.start()


    def one_rows(index, carry):
        part = index % parts
        first = pl.multiple_of(index // parts * 16, 16)
        values = [kept_ref[parts * j + part, pl.ds(first, 16), :] for j in range(RADIX)]
        bins = real_fourier(values)
        rows = pl.ds(pl.multiple_of(base + first, 16), 16)
        for group in range(GROUPS):
            pair = (bins[0][0], bins[GROUPS][0]) if group == 0 else bins[group]
            for half in range(2):
                lanes = pl.ds(pl.multiple_of(half * span + part * LANES, LANES), LANES)
                top = pair[half].astype(jnp.bfloat16)
                high_ref[group, rows, lanes] = top
                low_ref[group, rows, lanes] = (pair[half] - top.astype(jnp.float32)).astype(jnp.bfloat16)
        return carry

    lax.fori_loop(0, parts * inputs * frames // 16, one_rows, 0, unroll=8)

    @pl.when(step == steps - 1)
    def _():
        copy.wait()

        def one_group(group, carry):
            top, rest = high_ref[group], low_ref[group]
            total = jnp.dot(top, table_ref[group, 0], preferred_element_type=jnp.float32)
            total = total + jnp.dot(rest, table_ref[group, 0], preferred_element_type=jnp.float32)
            total = total + jnp.dot(top, table_ref[group, 1], preferred_element_type=jnp.float32)
            spec_ref[group] = total
            return carry

        lax.fori_loop(0, GROUPS, one_group, 0, unroll=GROUPS)
        owners = out_ref.shape[0]
        slots = GROUPS
        run = LANES // slots

        def one_part(index, carry):
            first = pl.multiple_of(index * 16, 16)
            slot = lax.broadcasted_iota(jnp.int32, (16, LANES), 1) // run
            picks = [(slot // (1 << bit)) % 2 == 1 for bit in range(3)]
            for kind in range(2):
                for block in range(owners // slots):
                    lanes = pl.ds((kind * (owners // slots) + block) * LANES, LANES)
                    now = [spec_ref[group, pl.ds(first, 16), lanes] for group in range(GROUPS)]
                    for bit in range(3):
                        now = [jnp.where(picks[bit], now[(e - (1 << bit)) % slots], now[e]) for e in range(slots)]
                    for inside in range(slots):
                        out_ref[block * slots + inside, pl.ds(first, 16), pl.ds(kind * LANES, LANES)] = now[inside].astype(jnp.bfloat16)
            return carry

        lax.fori_loop(0, out_ref.shape[1] // 16, one_part, 0, unroll=4)
        if following:
            store.wait()


def filter_bank(samples, history, coefficients, table, first, count, owners, following):
    _, frames, length = samples.shape
    steps = count // ROWS
    rows = count * frames
    offset = first // ROWS
    in_specs = [
        pl.BlockSpec((ROWS, frames, length), lambda i: (i + offset, 0, 0)),
        pl.BlockSpec(coefficients.shape, lambda i: (0, 0), pipeline_mode=pl.Buffered(1)),
        pl.BlockSpec(memory_space=pl.ANY),
        pl.BlockSpec(memory_space=pl.ANY),
    ]
    out_specs = [pl.BlockSpec((owners, rows, 2 * LANES), lambda i: (0, 0, 0), pipeline_mode=pl.Buffered(1))]
    out_shape = [jax.ShapeDtypeStruct((owners, rows, 2 * LANES), jnp.bfloat16)]
    operands = [samples, coefficients, table, history]
    if following:
        in_specs.append(pl.BlockSpec(memory_space=pl.ANY))
        out_specs.append(pl.BlockSpec(memory_space=pl.ANY))
        out_shape.append(jax.ShapeDtypeStruct((following[1], frames, length), samples.dtype))
        operands.append(samples)
    return pl.pallas_call(
        functools.partial(filter_bank_kernel, steps, following),
        out_shape=out_shape,
        grid=(steps,),
        in_specs=in_specs,
        out_specs=out_specs,
        scratch_shapes=[
            pltpu.VMEM((steps, ROWS, frames, length), jnp.bfloat16),
            pltpu.VMEM((2 * ROWS * frames, LANES), jnp.float32),
            pltpu.VMEM((length // LANES, ROWS * frames, LANES), jnp.float32),
            pltpu.VMEM((GROUPS, rows, 2 * length // RADIX), jnp.bfloat16),
            pltpu.VMEM((GROUPS, rows, 2 * length // RADIX), jnp.bfloat16),
            pltpu.VMEM((GROUPS, rows, 2 * owners * LANES // GROUPS), jnp.float32),
            pltpu.VMEM(table.shape, jnp.bfloat16),
            pltpu.SemaphoreType.DMA((steps + 3,)),
        ]
        + ([pltpu.VMEM((following[1], frames, length), samples.dtype)] if following else []),
        compiler_params=pltpu.CompilerParams(vmem_limit_bytes=63 * MIB),
        cost_estimate=pl.CostEstimate(flops=10**11, bytes_accessed=16 * MIB, transcendentals=0),
        name="filter_bank",
    )(*operands)


def cut_kernel(in_ref, out_ref):
    out_ref[...] = in_ref[...]


def cut(samples, first, count):
    block = (ROWS, *samples.shape[1:])
    return pl.pallas_call(
        cut_kernel,
        out_shape=jax.ShapeDtypeStruct((count, *samples.shape[1:]), samples.dtype),
        grid=(count // ROWS,),
        in_specs=[pl.BlockSpec(block, lambda i: (i + first // ROWS, 0, 0))],
        out_specs=pl.BlockSpec(block, lambda i: (i, 0, 0)),
        cost_estimate=pl.CostEstimate(flops=0, bytes_accessed=4 * MIB, transcendentals=0),
        name="cut",
    )(samples)


def turn_kernel(frames, in_ref, out_ref, work_ref):
    blocks, rows, _ = in_ref.shape
    count = rows // frames

    def one_input(i, carry):
        first = pl.multiple_of(i * frames, frames)
        pieces = [
            in_ref[t, pl.ds(first, frames), pl.ds(kind * LANES, LANES)]
            for kind in range(2)
            for t in range(blocks)
        ]
        square = jnp.concatenate(pieces, axis=0).astype(jnp.float32)
        work_ref[pl.ds(i, LANES, stride=count), :] = square.T
        return carry

    lax.fori_loop(0, count, one_input, 0, unroll=count)
    out_ref[...] = work_ref[...].reshape(LANES, count, LANES).astype(jnp.bfloat16)


def turn(arrived, sets, frames):
    sources, rows, _ = arrived.shape
    blocks = sources // sets
    count = rows // frames
    return pl.pallas_call(
        functools.partial(turn_kernel, frames),
        out_shape=jax.ShapeDtypeStruct((LANES, sets * count, LANES), jnp.bfloat16),
        grid=(sets,),
        in_specs=[pl.BlockSpec((blocks, rows, 2 * LANES), lambda z: (z, 0, 0))],
        out_specs=pl.BlockSpec((LANES, count, LANES), lambda z: (0, z, 0)),
        scratch_shapes=[pltpu.VMEM((LANES * count, LANES), jnp.float32)],
        compiler_params=pltpu.CompilerParams(vmem_limit_bytes=20 * MIB),
        cost_estimate=pl.CostEstimate(flops=4 * arrived.size, bytes_accessed=4 * arrived.size, transcendentals=0),
        name="turn",
    )(arrived)


def correlate_kernel(counts, sets, scale, order_ref, *refs):
    *in_refs, out_hbm, kept_ref, sems = refs
    _, many, held, width, _ = kept_ref.shape
    step = pl.program_id(0)
    slot = step % 2

    def copies(of_step, of_slot):
        return [
            pltpu.make_async_copy(
                kept_ref.at[of_slot, k], out_hbm.at[:, order_ref[many * of_step + k]], sems.at[of_slot, k]
            )
            for k in range(many)
        ]

    @pl.when(step >= 2)
    def _():
        for copy in copies(step - 2, slot):
            copy.wait()

    row = lax.broadcasted_iota(jnp.int32, (width, width), 0)
    col = lax.broadcasted_iota(jnp.int32, (width, width), 1)
    for k in range(many):
        for u in range(held):
            joined = jnp.concatenate(
                [
                    in_ref[held * k + u, pl.ds(z * count, count), :]
                    for z in range(sets)
                    for in_ref, count in zip(in_refs, counts)
                ],
                axis=0,
            )
            turned = jnp.concatenate([joined[:, LANES // 2 :], -joined[:, : LANES // 2]], axis=1)
            both = lax.dot_general(
                jnp.concatenate([joined, turned], axis=0),
                joined,
                (((1,), (1,)), ((), ())),
                preferred_element_type=jnp.float32,
            )
            kept_ref[slot, k, u] = jnp.where(row <= col, both[:width], both[width:]) * scale
    for copy in copies(step, slot):
        copy.start()

    @pl.when(step == pl.num_programs(0) - 1)
    def _():
        for copy in copies(step - 1, 1 - slot) + copies(step, slot):
            copy.wait()


def correlate_all(turned, counts, sets, order, scale):
    channels = turned[0].shape[0]
    held = channels // RADIX
    width = sets * sum(counts)
    many = 4
    out = pl.pallas_call(
        functools.partial(correlate_kernel, counts, sets, scale),
        out_shape=jax.ShapeDtypeStruct((held, RADIX, width, width), jnp.float32),
        grid_spec=pltpu.PrefetchScalarGridSpec(
            num_scalar_prefetch=1,
            grid=(RADIX // many,),
            in_specs=[
                pl.BlockSpec((many * held, sets * count, LANES), lambda s, order: (s, 0, 0)) for count in counts
            ],
            out_specs=pl.BlockSpec(memory_space=pl.ANY),
            scratch_shapes=[
                pltpu.VMEM((2, many, held, width, width), jnp.float32),
                pltpu.SemaphoreType.DMA((2, many)),
            ],
        ),
        compiler_params=pltpu.CompilerParams(vmem_limit_bytes=36 * MIB),
        cost_estimate=pl.CostEstimate(
            flops=4 * channels * width * width * LANES, bytes_accessed=40 * MIB, transcendentals=0
        ),
        name="correlate",
    )(order, *turned)
    return out.reshape(channels, width, width)


def plan(in_dev):
    units = in_dev // ROWS
    return [ROWS * size for size in (1, 2, 2, units - 5)]


def fast(samples, coefficients):
    in_dev, frames, length = samples.shape
    everyone = ("inp", "tm", "pol")
    owners = lax.axis_size(everyone)
    sets = lax.axis_size("inp")
    total_frames = frames * owners // sets
    table = jnp.asarray(fourier_tables(length, owners))
    counts = plan(in_dev)
    starts = [sum(counts[:k]) for k in range(len(counts))]
    slot = lax.axis_index(everyone) % GROUPS
    steps = jnp.arange(RADIX, dtype=jnp.int32)
    group, side = (slot - steps // 2) % GROUPS, steps % 2
    order = jnp.where(group == 0, side * GROUPS, jnp.where(side == 0, group, RADIX - group)).astype(jnp.int32)
    last = len(counts) - 1
    parts = list(zip(starts, counts))
    histories = [from_behind(samples[: counts[0]], ("tm", "pol"), 1)]
    piece, histories[0] = lax.optimization_barrier((cut(samples, *parts[1]), histories[0]))
    histories.append(from_behind(piece, ("tm", "pol"), 1))
    turned = []
    for k in range(last + 1):
        following = parts[k + 2] if k + 2 <= last else None
        spectra, *pieces = filter_bank(
            samples, histories[k], coefficients, table, starts[k], counts[k], owners, following
        )
        if following:
            piece = pieces[0]
            if k > 0:
                piece, arrived = lax.optimization_barrier((piece, arrived))
            piece, histories[k + 1] = lax.optimization_barrier((piece, histories[k + 1]))
            histories.append(from_behind(piece, ("tm", "pol"), 1))
        if k > 0:
            turned.append(turn(arrived, sets, frames))
        arrived = lax.all_to_all(spectra, everyone, 0, 0, tiled=True)
    turned.append(turn(arrived, sets, frames))
    return correlate_all(turned, counts, sets, order, 1.0 / total_frames)


def per_device(samples, coefficients):
    in_dev, frames, length = samples.shape
    taps = coefficients.shape[0]
    owners = lax.axis_size(("inp", "tm", "pol"))
    blocks = lax.axis_size(("tm", "pol"))
    fits = (
        frames == 16
        and taps <= frames + 1
        and in_dev % (4 * ROWS) == 0
        and length == 2 * LANES * owners
        and length % (RADIX * LANES) == 0
        and owners % GROUPS == 0
        and 2 * blocks * frames == LANES
    )
    return fast(samples, coefficients) if fits else general(samples, coefficients)


def solution(mesh):
    placed = (P(("grp", "inp"), ("tm", "pol"), None), P())
    return jax.shard_map(
        per_device,
        mesh=mesh,
        in_specs=placed,
        out_specs=P(("grp", "inp", "tm", "pol"), None, None),
        check_vma=False,
    )
```
